32 devices in a mesh: batch: 8 (over z, x), ctx: 4 (over y, core).
Axes of the slice: x: 2, y: 2, z: 4, core: 2. Of those that a mesh axis runs over, the one named last changes fastest.
Arguments:
- tokens: bfloat16 [8, 1024, 2048], P('batch', 'ctx'), may hold values from -6 to 6
- segment_ids: int32 [8, 1024], P('batch', 'ctx'), may hold values from 0 to 7, never falling along the last dimension, each value on 1 to 512 neighbouring positions
- valid_mask: int32 [8, 1024], P('batch', 'ctx'), may hold values from 0 to 1, as said below
- teacher: bfloat16 [8, 1024, 2048], P('batch', 'ctx'), may hold values from -6 to 6
- mixer_in: bfloat16 [2048, 6704], P(('batch', 'ctx')), may hold values from -0.125 to 0.125
- mixer_out: bfloat16 [3072, 2048], P(('batch', 'ctx')), may hold values from -0.0012207031 to 0.0012207031
- query_weight: bfloat16 [2048, 1024], P(('batch', 'ctx')), may hold values from -0.125 to 0.125
- key_value_weight: bfloat16 [2048, 512], P(('batch', 'ctx')), may hold values from -0.125 to 0.125
- output_weight: bfloat16 [1024, 2048], P(('batch', 'ctx')), may hold values from -1.5 to 1.5
- gate_up: bfloat16 [2048, 8192], P(('batch', 'ctx')), may hold values from -0.125 to 0.125
- down_weight: bfloat16 [4096, 2048], P(('batch', 'ctx')), may hold values from -0.09375 to 0.09375
- norm_first: float32 [2048], replicated, may hold values from 0.5 to 1.5
- norm_second: float32 [2048], replicated, may hold values from 0.5 to 1.5
- conv_taps: float32 [4, 3584], replicated, may hold values from -3 to 3
- decay_log: float32 [48], replicated, may hold values from -7.6 to -3
- skip_gain: float32 [48], replicated, may hold values from 0.5 to 1.5
- step_bias: float32 [48], replicated, may hold values from -2 to 0.5
Outputs:
- output: bfloat16 [8, 1024, 2048], P('batch', 'ctx')
- loss_value: float32 [], replicated
- grad_tokens: float32 [8, 1024, 2048], P('batch', 'ctx')
- grad_mixer_in: float32 [2048, 6704], P(('batch', 'ctx'))
- grad_mixer_out: float32 [3072, 2048], P(('batch', 'ctx'))
- grad_query_weight: float32 [2048, 1024], P(('batch', 'ctx'))
- grad_keyval_weight: float32 [2048, 512], P(('batch', 'ctx'))
- grad_output_weight: float32 [1024, 2048], P(('batch', 'ctx'))
- grad_gate_up: float32 [2048, 8192], P(('batch', 'ctx'))
- grad_down_weight: float32 [4096, 2048], P(('batch', 'ctx'))
- grad_norm_first: float32 [2048], replicated
- grad_norm_second: float32 [2048], replicated
- grad_conv_taps: float32 [4, 3584], replicated
- grad_decay_log: float32 [48], replicated
- grad_skip_gain: float32 [48], replicated
- grad_step_bias: float32 [48], replicated
The draws below stay inside these ranges and needn't reach their ends.
Inputs may be any that keep to these rules, and one draw needn't show every extreme that they name: `segment_ids`: within a sequence the ids never fall; each document is 1 to 512 tokens long and one is exactly that long. `valid_mask`: the share of ones rises from about 0.3 in the first sequence to about 0.95 in the last.
All inputs are finite; a program needn't handle non-finite values.
Results may differ from the reference program's by a relative error of at most 0.012.
Values may be sent and summed in bfloat16 or wider, within the bound.
No kernel may reach another device: no remote copies, remote signals or barrier semaphores. Data moves between devices by JAX's collectives and lax.ppermute only.
A program may use at most 448 MiB of HBM per device.

```python
import math
import jax
import jax.numpy as jnp
import numpy as np
from jax import lax

MODEL_WIDTH = 2048
H_M = 48
P_SIZE = 64
N = 256
QUERY_HEADS = 8
KEY_VALUE_HEADS = 2
HEAD_SIZE = 128
FF = 4096
TAPS = 4
DOCS = 8
TOK_DEV = 256
DI = 3072
SEQUENCE_TOKENS = 1024
SEQS = 8
TOKENS = 8192


def draw_valid_mask(key, part):
    rolls = jax.random.randint(key, (SEQS, SEQUENCE_TOKENS), 0, 1000)
    level = 300 + 650 * jnp.arange(SEQS, dtype=jnp.int32) // max(SEQS - 1, 1)
    return (rolls < level[:, None]).astype(jnp.int32)


def shard_levels(key, dims, cuts, least, largest):
    loudness = 1.0
    for position, parts in cuts:
        draws = jax.random.uniform(jax.random.fold_in(jax.random.fold_in(key, 6), position), (parts,), jnp.float32, least / len(cuts), largest / len(cuts))
        loudness = loudness * jnp.repeat(jnp.exp(draws), dims[position] // parts).reshape((-1,) + (1,) * (len(dims) - 1 - position))
    return loudness


def split_up(number_of, total, limit, lean):
    portions = [(1 << 20) // math.isqrt(rank ** lean) + 1 for rank in range(2, number_of + 1)]
    rest, counts = total - limit - (number_of - 1), [1] * (number_of - 1)
    while rest > 0:
        movable = [i for i in range(number_of - 1) if counts[i] < limit]
        pool, remaining = sum([portions[i] for i in movable]), rest
        for i in movable:
            addition = min(limit - counts[i], max(1, remaining * portions[i] // pool), rest)
            counts[i] = counts[i] + addition
            rest = rest - addition
    return np.array([limit] + counts)


def uneven_parts(own_key, amount, total, bound, slope):
    if amount == 2:
        one = jax.random.randint(own_key, (), max(1, total - bound), min(bound, total - 1) + 1)
        return jnp.stack([one, total - one])
    lengths = jnp.asarray(split_up(amount, total, bound, slope), jnp.int32)
    pairs = (amount - 1) // 2
    source_of, receiver = lengths[1:1 + 2 * pairs:2], lengths[2:2 + 2 * pairs:2]
    room = jnp.minimum(source_of - 1, bound - receiver)
    moved = jax.random.randint(jax.random.fold_in(own_key, 1), (pairs,), 0, 1 << 20) % (room + 1)
    lengths = lengths.at[1:1 + 2 * pairs:2].set(source_of - moved).at[2:2 + 2 * pairs:2].set(receiver + moved)
    return lengths[jax.random.permutation(jax.random.fold_in(own_key, 2), amount)]


def centred(stream_key, extent, scale, bound, cuts=(), kind=jnp.bfloat16):
    level = shard_levels(stream_key, extent, cuts, -0.22, 0.18) if cuts else 1.0
    values = jax.random.normal(stream_key, extent, jnp.float32) * scale * level
    return jnp.minimum(jnp.maximum(values, -bound), bound).astype(kind)


def setup_inputs(seed: int = 0) -> dict:
    key_of = jax.random.split(jax.random.key(seed), 18)
    return {
        "tokens": centred(key_of[0], (SEQS, SEQUENCE_TOKENS, MODEL_WIDTH), 1.0, 6.0, ((0, 8), (1, 4))),
        "segment_ids": jax.vmap(lambda own: jnp.searchsorted(jnp.cumsum(uneven_parts(own, DOCS, SEQUENCE_TOKENS, SEQUENCE_TOKENS // 2, 2)), jnp.arange(SEQUENCE_TOKENS), side="right"))(jax.random.split(key_of[1], SEQS)).reshape((SEQS, SEQUENCE_TOKENS)).astype(jnp.int32),
        "valid_mask": draw_valid_mask(jax.random.fold_in(key_of[17], 71), 0),
        "teacher": centred(key_of[3], (SEQS, SEQUENCE_TOKENS, MODEL_WIDTH), 1.0, 6.0, ((0, 8), (1, 4))),
        "mixer_in": centred(key_of[4], (MODEL_WIDTH, 2 * DI + 2 * N + H_M), MODEL_WIDTH ** -0.5, 0.125, ((0, 32),)),
        "mixer_out": centred(key_of[5], (DI, MODEL_WIDTH), (DI * N * 32) ** -0.5, 0.0012207031, ((0, 32),)),
        "query_weight": centred(key_of[6], (MODEL_WIDTH, QUERY_HEADS * HEAD_SIZE), MODEL_WIDTH ** -0.5, 0.125, ((0, 32),)),
        "key_value_weight": centred(key_of[7], (MODEL_WIDTH, 2 * KEY_VALUE_HEADS * HEAD_SIZE), MODEL_WIDTH ** -0.5, 0.125, ((0, 32),)),
        "output_weight": centred(key_of[8], (QUERY_HEADS * HEAD_SIZE, MODEL_WIDTH), (QUERY_HEADS * HEAD_SIZE // 64) ** -0.5, 1.5, ((0, 32),)),
        "gate_up": centred(key_of[9], (MODEL_WIDTH, 2 * FF), MODEL_WIDTH ** -0.5, 0.125, ((0, 32),)),
        "down_weight": centred(key_of[10], (FF, MODEL_WIDTH), FF ** -0.5, 0.09375, ((0, 32),)),
        "norm_first": jnp.clip(1.0 + 0.1 * jax.random.normal(key_of[11], (MODEL_WIDTH,), jnp.float32), 0.5, 1.5),
        "norm_second": jnp.clip(1.0 + 0.1 * jax.random.normal(key_of[12], (MODEL_WIDTH,), jnp.float32), 0.5, 1.5),
        "conv_taps": centred(key_of[13], (TAPS, DI + 2 * N), 0.5, 3.0, (), jnp.float32),
        "decay_log": jnp.clip(jax.random.uniform(key_of[14], (H_M,), jnp.float32, -7.6, -3.0), -7.6, -3.0),
        "skip_gain": jnp.clip(jax.random.uniform(key_of[15], (H_M,), jnp.float32, 0.5, 1.5), 0.5, 1.5),
        "step_bias": jnp.clip(jax.random.uniform(key_of[16], (H_M,), jnp.float32, -2.0, 0.5), -2.0, 0.5),
    }


NORM_EPSILON = 1e-05
ROPE_BASE = 1000000.0
HIGHEST = lax.Precision.HIGHEST

@jax.custom_vjp
def lower_bound(v):
    return lax.optimization_barrier(v.astype(jnp.bfloat16)).astype(jnp.float32)

@jax.custom_vjp
def low_back(v):
    return v

def low_keep(v):
    return (lower_bound(v), None)

def low_pass(kept, grad):
    return (grad,)

def back_keep(v):
    return (v, None)

def back_low(kept, grad):
    return (lower_bound(grad),)
lower_bound.defvjp(low_keep, low_pass)
low_back.defvjp(back_keep, back_low)

def matmul(left, right):
    return jnp.dot(left, right, precision=HIGHEST, preferred_element_type=jnp.float32)

def rms_norm(value_rows, gain):
    return value_rows * lax.rsqrt(lax.optimization_barrier(jnp.mean(value_rows * value_rows, axis=-1, keepdims=True)) + NORM_EPSILON) * gain

def apply_rotary(heads, token_position):
    half = HEAD_SIZE // 2
    inverse = ROPE_BASE ** (-(jnp.arange(half, dtype=jnp.float32) * 2.0) / HEAD_SIZE)
    angle = token_position.astype(jnp.float32)[:, None] * inverse[None, :]
    cosine = jnp.cos(angle)[:, None, :]
    sine = jnp.sin(angle)[:, None, :]
    leading_part = heads[..., :half]
    second = heads[..., half:]
    return jnp.concatenate([leading_part * cosine - second * sine, second * cosine + leading_part * sine], axis=-1)

def conv_segments(padded, padded_segs, segments, taps):
    count_rows = segments.shape[0]
    total = jnp.zeros((count_rows, padded.shape[1]), jnp.float32)
    for lag in range(TAPS):
        begin = TAPS - 1 - lag
        shifted = padded[begin:begin + count_rows]
        keep = (padded_segs[begin:begin + count_rows] == segments).astype(jnp.float32)[:, None]
        total = total + taps[lag] * shifted * keep
    return total

def ssd_states(xs, bmat, decay, step, segments, seg_before):
    cumulative = jnp.cumsum(decay, axis=0)
    weight = jnp.exp(cumulative[-1][None, :] - cumulative) * (segments == segments[-1]).astype(jnp.float32)[:, None] * step
    tail_state = jnp.einsum('shp,sn->hpn', weight[:, :, None] * xs, bmat, precision=HIGHEST)
    through = jnp.exp(cumulative[-1]) * (segments[-1] == seg_before).astype(jnp.float32)
    return (tail_state, through)

def ssd_output(xs, bmat, cmat, decay, step, segments, seg_before, state_in):
    count_rows = xs.shape[0]
    cumulative = jnp.cumsum(decay, axis=0)
    order = jnp.arange(count_rows)
    allowed = (segments[:, None] == segments[None, :]) & (order[:, None] >= order[None, :])
    spread = cumulative.T[:, :, None] - cumulative.T[:, None, :]
    kernel = jnp.exp(jnp.where(allowed[None], spread, -1e+30))
    inner = jnp.dot(cmat, bmat.T, precision=HIGHEST, preferred_element_type=jnp.float32)
    mixing = kernel * inner[None] * step.T[:, None, :]
    local = jnp.einsum('hts,shp->thp', mixing, xs, precision=HIGHEST)
    carried = jnp.einsum('hpn,tn->thp', state_in, cmat, precision=HIGHEST)
    keep = (segments == seg_before).astype(jnp.float32)
    return local + (jnp.exp(cumulative) * keep[:, None])[:, :, None] * carried

def ssd_sequence(xs, bmat, cmat, decay, step, segments):
    blocks = SEQUENCE_TOKENS // TOK_DEV

    def one_block(carry, piece):
        state, seg_before = carry
        xs_b, b_b, c_b, decay_b, step_b, seg_b = piece
        tail_state, through = ssd_states(xs_b, b_b, decay_b, step_b, seg_b, seg_before)
        result = ssd_output(xs_b, b_b, c_b, decay_b, step_b, seg_b, seg_before, state)
        return ((tail_state + through[:, None, None] * state, seg_b[-1]), result)
    pieces = tuple((v.reshape((blocks, TOK_DEV) + v.shape[1:]) for v in (xs, bmat, cmat, decay, step, segments)))
    start_state = (jnp.zeros((H_M, P_SIZE, N), jnp.float32), jnp.array(-1, jnp.int32))
    final_carry, results = lax.scan(jax.checkpoint(one_block), start_state, pieces)
    return results.reshape(SEQUENCE_TOKENS, H_M, P_SIZE)

def attention_sequence(query_rows, key_rows, value_rows, segments):
    document_span = SEQUENCE_TOKENS if SEQUENCE_TOKENS <= 512 else 512
    scale = HEAD_SIZE ** (-0.5)
    query_per_group = QUERY_HEADS // KEY_VALUE_HEADS

    def one_block(leading_part):
        query_block_rows = lax.dynamic_slice_in_dim(query_rows, leading_part, document_span, 0).reshape(document_span, KEY_VALUE_HEADS, query_per_group, HEAD_SIZE)
        block_seg = lax.dynamic_slice_in_dim(segments, leading_part, document_span, 0)
        scores = low_back(jnp.einsum('tkgd,skd->kgts', query_block_rows, key_rows, precision=HIGHEST) * scale)
        places = leading_part + jnp.arange(document_span, dtype=jnp.int32)
        allowed = (places[:, None] >= jnp.arange(SEQUENCE_TOKENS, dtype=jnp.int32)[None, :]) & (block_seg[:, None] == segments[None, :])
        scores = jnp.where(allowed, scores, -1e+30)
        probs = jax.nn.softmax(scores, axis=-1)
        result = jnp.einsum('kgts,skd->tkgd', lower_bound(probs), value_rows, precision=HIGHEST)
        return result.reshape(document_span, QUERY_HEADS * HEAD_SIZE)
    firsts = (jnp.arange(SEQUENCE_TOKENS // document_span) * document_span).astype(jnp.int32)
    return lax.map(jax.checkpoint(one_block), firsts).reshape(SEQUENCE_TOKENS, QUERY_HEADS * HEAD_SIZE)

def sequence_objective(residual, weights, segments, valid, target, count):
    mixer_in, mixer_out, query_weight, key_value_weight, output_weight, gate_up, down_weight, norm_first, norm_second, conv_taps, decay_log, skip_gain, step_bias = weights
    normed = lower_bound(rms_norm(residual, norm_first))
    mixed = low_back(matmul(normed, mixer_in))
    gate_z = mixed[:, :DI]
    conv_in = lower_bound(mixed[:, DI:2 * DI + 2 * N])
    step_raw = mixed[:, 2 * DI + 2 * N:]
    padded = jnp.concatenate([jnp.zeros((TAPS - 1, DI + 2 * N), jnp.float32), conv_in], axis=0)
    padded_segs = jnp.concatenate([jnp.full((TAPS - 1,), -1, jnp.int32), segments])
    activated = jax.nn.silu(conv_segments(padded, padded_segs, segments, conv_taps))
    xs = activated[:, :DI].reshape(SEQUENCE_TOKENS, H_M, P_SIZE)
    bmat = activated[:, DI:DI + N]
    cmat = activated[:, DI + N:]
    step = jax.nn.softplus(step_raw + step_bias)
    decay = -jnp.exp(decay_log) * step
    ssm_y = ssd_sequence(xs, bmat, cmat, decay, step, segments) + skip_gain[:, None] * xs
    gated = lower_bound(ssm_y.reshape(SEQUENCE_TOKENS, DI) * jax.nn.silu(gate_z))
    mixer_branch = low_back(matmul(gated, mixer_out))
    token_position = jnp.arange(SEQUENCE_TOKENS, dtype=jnp.int32)
    query_raw = low_back(matmul(normed, query_weight)).reshape(SEQUENCE_TOKENS, QUERY_HEADS, HEAD_SIZE)
    key_value_projected = low_back(matmul(normed, key_value_weight))
    query_rows = lower_bound(apply_rotary(query_raw, token_position))
    key_rows = lower_bound(apply_rotary(key_value_projected[:, :KEY_VALUE_HEADS * HEAD_SIZE].reshape(SEQUENCE_TOKENS, KEY_VALUE_HEADS, HEAD_SIZE), token_position))
    value_rows = lower_bound(key_value_projected[:, KEY_VALUE_HEADS * HEAD_SIZE:].reshape(SEQUENCE_TOKENS, KEY_VALUE_HEADS, HEAD_SIZE))
    attended = lower_bound(low_back(attention_sequence(query_rows, key_rows, value_rows, segments)))
    attend_branch = low_back(matmul(attended, output_weight))
    hidden_one = residual + mixer_branch + attend_branch
    normed_two = lower_bound(rms_norm(hidden_one, norm_second))
    gateup = low_back(matmul(normed_two, gate_up))
    hidden = lower_bound(jax.nn.silu(gateup[:, :FF]) * gateup[:, FF:])
    ffn_branch = low_back(matmul(hidden, down_weight))
    final = hidden_one + ffn_branch
    error = final - target
    squares = jnp.sum(valid * lax.optimization_barrier(jnp.sum(error * error, axis=1)))
    return (squares * (TOKENS / (2.0 * count)), (final, squares))

def reference(tokens, segment_ids, valid_mask, teacher, mixer_in, mixer_out, query_weight, key_value_weight, output_weight, gate_up, down_weight, norm_first, norm_second, conv_taps, decay_log, skip_gain, step_bias):
    weights = tuple((v.astype(jnp.float32) for v in (mixer_in, mixer_out, query_weight, key_value_weight, output_weight, gate_up, down_weight, norm_first, norm_second, conv_taps, decay_log, skip_gain, step_bias)))
    count = jnp.sum(valid_mask.astype(jnp.float32))

    def one_sequence(totals, item):
        seq_tokens, seq_segs, seq_valid, seq_teacher = item

        def objective(residual, params):
            return sequence_objective(residual, params, seq_segs, seq_valid.astype(jnp.float32), seq_teacher.astype(jnp.float32), count)
        value, pullback, extra = jax.vjp(objective, seq_tokens.astype(jnp.float32), weights, has_aux=True)
        grad_residual, grad_weights = pullback(jnp.ones_like(value))
        totals = tuple((a + b for a, b in zip(totals, grad_weights)))
        final, squares = extra
        return (totals, (final.astype(jnp.bfloat16), grad_residual, squares))
    zeros = tuple((jnp.zeros_like(v) for v in weights))
    totals, outputs = lax.scan(one_sequence, zeros, (tokens, segment_ids, valid_mask, teacher))
    finals, grad_tokens, squares = outputs
    loss_value = jnp.sum(squares) / (MODEL_WIDTH * count)
    return (finals, loss_value, grad_tokens, totals[0], totals[1], totals[2], totals[3], totals[4], totals[5], totals[6], totals[7], totals[8], totals[9], totals[10], totals[11], totals[12])
```

```python
import functools

import jax
import jax.numpy as jnp
from jax import lax
from jax.experimental import pallas as pl
from jax.experimental.pallas import tpu as pltpu
from jax.sharding import PartitionSpec as P

MODEL_WIDTH = 2048
H_M = 48
P_SIZE = 64
N = 256
QUERY_HEADS = 8
KEY_VALUE_HEADS = 2
HEAD_SIZE = 128
FF = 4096
TAPS = 4
DI = 3072

NC = 4
HEADS = H_M // NC
PAIRS = HEADS // 2
WX = DI // NC
WB = 2 * N // NC
WQ = QUERY_HEADS * HEAD_SIZE // NC
QH = QUERY_HEADS // NC
WF = FF // NC
CHUNK = 128

NORM_EPSILON = 1e-05
ROPE_BASE = 1000000.0
HIGHEST = lax.Precision.HIGHEST
F32 = jnp.float32
BF16 = jnp.bfloat16


def mm(left, right):
    return jnp.dot(left, right, preferred_element_type=F32)


def mm_tn(left, right):
    return lax.dot_general(left, right, (((0,), (0,)), ((), ())), preferred_element_type=F32)


def mm_nt(left, right):
    return lax.dot_general(left, right, (((1,), (1,)), ((), ())), preferred_element_type=F32)


def after(value, *deps):
    return lax.optimization_barrier((value,) + deps)[0]


def core_swap(value):
    return lax.ppermute(value, "ctx", [(i, i ^ 1) for i in range(NC)])


def y_swap(value):
    return lax.ppermute(value, "ctx", [(i, i ^ 2) for i in range(NC)])


class Ring:
    def __init__(self):
        self.n = lax.axis_size("batch")
        n = self.n
        order = list(range(0, n, 2)) + list(range(n - 1, 0, -2))
        self.up_pairs = [(order[i], order[(i + 1) % n]) for i in range(n)]
        self.down_pairs = [(order[(i + 1) % n], order[i]) for i in range(n)]
        b = lax.axis_index("batch")
        self.pos = jnp.where(b % 2 == 0, b // 2, n - 1 - b // 2)

    def up(self, value):
        return lax.ppermute(value, "batch", self.up_pairs)

    def down(self, value):
        return lax.ppermute(value, "batch", self.down_pairs)

    def owner(self, slot):
        p = (self.pos + slot + self.n) % self.n
        return jnp.where(p < self.n // 2, 2 * p, 2 * (self.n - 1 - p) + 1)


class Order:
    def __init__(self, token):
        self.token = token

    def gate(self, *values):
        out = lax.optimization_barrier(values + (self.token,))
        self.token = out[-1]
        return out[:-1]


class GatherRun:
    def __init__(self, ring, order, block, place=lambda b: b):
        self.ring, self.order, self.place = ring, order, place
        self.rows, cols = block.shape
        (block,) = order.gate(block)
        self.down, self.up = ring.down(block), ring.up(block)
        self.whole = jnp.zeros((ring.n * self.rows, cols), block.dtype)
        self.put(block, 0)
        self.step, self.over = 1, False

    def put(self, part, slot, offset=0):
        at = self.place(self.ring.owner(slot)) * self.rows + offset
        self.whole = lax.dynamic_update_slice(self.whole, part, (at, 0))

    def turn(self, others):
        ring, far, half = self.ring, self.ring.n // 2, self.rows // 2
        down, up, *others = self.order.gate(self.down, self.up, *others)
        if self.step < far:
            if self.step + 1 < far:
                self.down, self.up = ring.down(down), ring.up(up)
            else:
                self.down, self.up = ring.down(down[half:]), ring.up(up[:half])
            self.put(down, self.step)
            self.put(up, -self.step)
        else:
            self.put(up, far)
            self.put(down, far, half)
            self.over = True
        self.step += 1
        return others


class ReduceRun:
    def __init__(self, ring, order, part):
        self.ring, self.order, self.part = ring, order, part
        far = part(ring.n // 2).astype(BF16)
        (far,) = order.gate(far)
        self.half = far.shape[0] // 2
        self.up, self.down = ring.up(far[: self.half]), ring.down(far[self.half :])
        self.step, self.over = ring.n // 2 - 1, False

    def turn(self, others):
        half = self.half
        up, down, *others = self.order.gate(self.up, self.down, *others)
        if self.step == 0:
            self.result = self.part(0) + up.astype(F32) + down.astype(F32)
            self.over = True
            return others
        a, b = self.part(self.step), self.part(-self.step)
        if self.step == self.ring.n // 2 - 1:
            a = jnp.concatenate([a[:half] + up.astype(F32), a[half:]], axis=0)
            b = jnp.concatenate([b[:half], b[half:] + down.astype(F32)], axis=0)
        else:
            a = a + up.astype(F32)
            b = b + down.astype(F32)
        self.up, self.down = self.ring.up(a.astype(BF16)), self.ring.down(b.astype(BF16))
        self.step -= 1
        return others


def sum_everywhere(value, batch):
    value = value + core_swap(value)
    value = value + y_swap(value)
    bit = 1
    while bit < batch:
        value = value + lax.ppermute(value, "batch", [(i, i ^ bit) for i in range(batch)])
        bit *= 2
    return value


class Spread:
    def __init__(self, parts, j):
        self.parts, self.j = parts, j
        self.got = y_swap(jnp.stack([parts[j ^ 2], parts[j ^ 3]]))

    def cross(self):
        self.across = core_swap(jnp.stack([self.parts[self.j ^ 1], self.got[1]]))

    def block(self):
        blocks = [self.parts[self.j], self.across[0], self.got[0], self.across[1]]
        whole = absolute(blocks, self.j)
        return whole.reshape(NC * whole.shape[1], whole.shape[2])


class Collect:
    def __init__(self, block, j):
        self.block, self.j = block, j
        self.got = core_swap(jnp.stack([block[j ^ 1], block[j ^ 3]]))

    def cross(self):
        self.far = y_swap(jnp.stack([self.block[self.j ^ 2], self.got[1]]))

    def result(self):
        whole = absolute([self.block[self.j], self.got[0], self.far[0], self.far[1]], self.j)
        return whole.astype(F32)


def absolute(blocks, j):
    whole = jnp.zeros((NC,) + blocks[0].shape, blocks[0].dtype)
    for k in range(NC):
        whole = lax.dynamic_update_slice(
            whole, blocks[k][None], (j ^ k,) + (0,) * blocks[0].ndim
        )
    return whole


def stacked(blocks):
    size = blocks[0].shape[0]
    whole = jnp.zeros((len(blocks) * size,) + blocks[0].shape[1:], blocks[0].dtype)
    for k, block in enumerate(blocks):
        whole = lax.dynamic_update_slice_in_dim(whole, block, k * size, 0)
    return whole


class Near:
    def __init__(self, own):
        self.own, self.far, self.next = own, y_swap(own), core_swap(own)

    def cross(self):
        self.last = core_swap(self.far)

    def blocks(self):
        return [self.own, self.next, self.far, self.last]


class NearSum:
    def __init__(self, part):
        third = core_swap(part(3).astype(BF16))
        self.second = y_swap((part(2) + third.astype(F32)).astype(BF16))
        self.first = core_swap(part(1).astype(BF16))
        self.near = part(0)

    def result(self):
        return self.near + self.first.astype(F32) + self.second.astype(F32)


def halves(first, second, lanes):
    return jnp.where(lanes < P_SIZE, first, second)


def kernel_of(colv, rowv, h, allowed):
    spread = colv[:, h : h + 1] - rowv[h : h + 1, :]
    return jnp.exp(jnp.where(allowed, spread, -1e30))


def chunk_mask(colv, rowv):
    shape = (CHUNK, CHUNK)
    rows = lax.broadcasted_iota(jnp.int32, shape, 0)
    cols = lax.broadcasted_iota(jnp.int32, shape, 1)
    same = colv[:, 4 * HEADS : 4 * HEADS + 1] == rowv[2 * HEADS : 2 * HEADS + 1, :]
    return same & (rows >= cols)


def ssd_forward_kernel(thr, x_ref, b_ref, c_ref, col_ref, row_ref, skip_ref, y_ref, st_ref, state):
    i = pl.program_id(0)

    @pl.when(i == 0)
    def _():
        state[...] = jnp.zeros_like(state)

    colv, rowv = col_ref[...], row_ref[...]
    b, c = b_ref[...].astype(BF16), c_ref[...].astype(BF16)
    allowed = chunk_mask(colv, rowv)
    inner = mm_nt(c, b)
    lanes = lax.broadcasted_iota(jnp.int32, (CHUNK, 2 * P_SIZE), 1)
    subs = lax.broadcasted_iota(jnp.int32, (2 * P_SIZE, N), 0)
    for p in range(PAIRS):
        span = slice(2 * P_SIZE * p, 2 * P_SIZE * (p + 1))
        x = x_ref[:, span]
        xb = x.astype(BF16)
        local = []
        for h in (2 * p, 2 * p + 1):
            mixing = kernel_of(colv, rowv, h, allowed) * inner * rowv[HEADS + h : HEADS + h + 1, :]
            local.append(mm(mixing.astype(BF16), xb))
        h = 2 * p

        def pick(base):
            return halves(
                colv[:, base + h : base + h + 1], colv[:, base + h + 1 : base + h + 2], lanes
            )

        held = state[span, :]
        hb = held.astype(BF16)
        st_ref[0, span, :] = hb
        y_ref[:, span] = (
            halves(local[0], local[1], lanes)
            + pick(HEADS) * mm_nt(c, hb)
            + skip_ref[:, span] * x
        )
        tail = mm_tn((pick(2 * HEADS) * x).astype(BF16), b)
        through = jnp.where(subs < P_SIZE, thr[i, h], thr[i, h + 1])
        state[span, :] = through * held + tail


def ssd_backward_kernel(first, *refs):
    (thr, g_ref, x_ref, b_ref, c_ref, col_ref, row_ref, skip_ref, st_ref), refs = refs[:9], refs[9:]
    if first:
        (dbc_in, dcol_in, _), refs = refs[:3], refs[3:]
    dx_ref, dbc_ref, dcol_ref, drow_ref, later = refs
    i = pl.num_programs(0) - 1 - pl.program_id(0)

    @pl.when(pl.program_id(0) == 0)
    def _():
        later[...] = jnp.zeros_like(later)

    colv, rowv = col_ref[...], row_ref[...]
    b, c = b_ref[...].astype(BF16), c_ref[...].astype(BF16)
    allowed = chunk_mask(colv, rowv)
    inner = mm_nt(c, b)
    lanes = lax.broadcasted_iota(jnp.int32, (CHUNK, 2 * P_SIZE), 1)
    subs = lax.broadcasted_iota(jnp.int32, (2 * P_SIZE, N), 0)
    last = lax.broadcasted_iota(jnp.int32, (CHUNK, 1), 0) == CHUNK - 1
    d_inner = jnp.zeros((CHUNK, CHUNK), F32)
    db = jnp.zeros((CHUNK, N), F32)
    dc = jnp.zeros((CHUNK, N), F32)
    dcol = dcol_in[...] if first else jnp.zeros((CHUNK, 128), F32)
    rows_out = []
    wide = lax.broadcasted_iota(jnp.int32, (CHUNK, 128), 1)
    for p in range(PAIRS // 2):
        span = slice(2 * P_SIZE * p, 2 * P_SIZE * (p + 1))
        x, g = x_ref[:, span], g_ref[:, span]
        xb, gb = x.astype(BF16), g.astype(BF16)
        h = 2 * (p + first)

        def pick(base):
            return halves(
                colv[:, base + h : base + h + 1], colv[:, base + h + 1 : base + h + 2], lanes
            )

        start = st_ref[0, span, :]
        ahead = later[span, :]
        ab = ahead.astype(BF16)
        reach, weight, bare = pick(HEADS), pick(2 * HEADS), pick(3 * HEADS)
        bs = mm_nt(b, ab)
        cs = mm_nt(c, start)
        xbs = x * bs
        carried = g * cs * reach
        stored = xbs * weight
        direct = xbs * bare
        product = ahead * start.astype(F32)
        local = []
        for q in (0, 1):
            hq = h + q
            mine = (lanes >= P_SIZE) if q else (lanes < P_SIZE)
            e = kernel_of(colv, rowv, hq, allowed)
            step = rowv[HEADS + hq : HEADS + hq + 1, :]
            d_mix = mm_nt(jnp.where(mine, g, 0.0).astype(BF16), xb)
            e_step = e * step
            local.append(mm_tn((e_step * inner).astype(BF16), gb))
            d_e = d_mix * e_step
            d_inner = d_inner + d_e
            total = d_e * inner
            rows_out.append(jnp.sum(d_mix * e * inner, axis=0, keepdims=True))
            stored_sum = jnp.sum(jnp.where(mine, stored, 0.0), axis=1, keepdims=True)
            d_cum = (
                jnp.sum(total, axis=1, keepdims=True)
                + jnp.sum(jnp.where(mine, carried - stored, 0.0), axis=1, keepdims=True)
            )
            mine_rows = (subs >= P_SIZE) if q else (subs < P_SIZE)
            end = jnp.sum(stored_sum) + thr[i, hq] * jnp.sum(jnp.where(mine_rows, product, 0.0))
            d_cum = d_cum + jnp.where(last, end, 0.0)
            d_step = jnp.sum(jnp.where(mine, direct, 0.0), axis=1, keepdims=True)
            dcol = jnp.where(wide == hq, d_cum, dcol)
            dcol = jnp.where(wide == HEADS + hq, d_step, dcol)
        gr = (reach * g).astype(BF16)
        dc = dc + mm(gr, start)
        db = db + mm((weight * x).astype(BF16), ab)
        dx_ref[:, span] = (
            halves(local[0], local[1], lanes) + weight * bs + skip_ref[:, span] * g
        )
        through = jnp.where(subs < P_SIZE, thr[i, h], thr[i, h + 1])
        later[span, :] = through * ahead + mm_tn(gr, c)
    di = d_inner.astype(BF16)
    db = db + mm_tn(di, c)
    dc = dc + mm(di, b)
    for q, value in enumerate((db[:, :WB], db[:, WB:], dc[:, :WB], dc[:, WB:])):
        dbc_ref[q] = value + dbc_in[q] if first else value
    dcol_ref[...] = dcol
    drow_ref[: len(rows_out), :] = jnp.concatenate(rows_out, axis=0)


def ssd_specs(chunks, flip, width, part):
    def at(i):
        return chunks - 1 - i if flip else i

    wide = pl.BlockSpec((CHUNK, width), lambda i: (at(i), part))
    mat = pl.BlockSpec((CHUNK, N), lambda i: (at(i), 0))
    col = pl.BlockSpec((CHUNK, 128), lambda i: (at(i), 0))
    row = pl.BlockSpec((32, CHUNK), lambda i: (0, at(i)))
    drow = pl.BlockSpec((8, CHUNK), lambda i: (0, at(i)))
    skip = pl.BlockSpec((1, width), lambda i: (0, part))
    states = pl.BlockSpec((1, width, N), lambda i: (at(i), part, 0))
    dbc = pl.BlockSpec((NC, CHUNK, WB), lambda i: (0, at(i), 0))
    thr = pl.BlockSpec(memory_space=pltpu.SMEM)
    return thr, wide, mat, col, row, drow, skip, states, dbc


def ssd_forward(thr, x, b, c, colv, rowv, skip):
    tokens = x.shape[0]
    chunks = tokens // CHUNK
    t, wide, mat, col, row, _, sk, states, _ = ssd_specs(chunks, False, WX, 0)
    return pl.pallas_call(
        ssd_forward_kernel,
        grid=(chunks,),
        in_specs=[t, wide, mat, mat, col, row, sk],
        out_specs=[wide, states],
        out_shape=[
            jax.ShapeDtypeStruct((tokens, WX), F32),
            jax.ShapeDtypeStruct((chunks, WX, N), BF16),
        ],
        scratch_shapes=[pltpu.VMEM((WX, N), F32)],
        compiler_params=pltpu.CompilerParams(
            dimension_semantics=("arbitrary",), vmem_limit_bytes=32 << 20
        ),
        name="ssd_forward",
    )(thr, x, b, c, colv, rowv, skip)


def ssd_backward(part, thr, g, x, b, c, colv, rowv, skip, states, earlier=()):
    tokens = x.shape[0]
    chunks = tokens // CHUNK
    t, wide, mat, col, row, drow, sk, st, dbc = ssd_specs(chunks, True, WX // 2, part)
    extra = [dbc, col, pl.BlockSpec(memory_space=pl.ANY)] if part else []
    return pl.pallas_call(
        functools.partial(ssd_backward_kernel, part * PAIRS // 2),
        grid=(chunks,),
        in_specs=[t, wide, wide, mat, mat, col, row, sk, st] + extra,
        out_specs=[wide, dbc, col, drow],
        out_shape=[
            jax.ShapeDtypeStruct((tokens, WX), F32),
            jax.ShapeDtypeStruct((NC, tokens, WB), F32),
            jax.ShapeDtypeStruct((tokens, 128), F32),
            jax.ShapeDtypeStruct((8, tokens), F32),
        ],
        scratch_shapes=[pltpu.VMEM((WX // 2, N), F32)],
        input_output_aliases={11: 0} if part else {},
        compiler_params=pltpu.CompilerParams(
            dimension_semantics=("arbitrary",), vmem_limit_bytes=40 << 20
        ),
        name="ssd_backward",
    )(thr, g, x, b, c, colv, rowv, skip, states, *earlier)


Q_BLOCK = 256
SCALE = HEAD_SIZE ** (-0.5)


def attention_probs(q, k, segc, segr, i):
    scores = mm_nt(q, k) * SCALE
    rows = lax.broadcasted_iota(jnp.int32, scores.shape, 0) + i * Q_BLOCK
    cols = lax.broadcasted_iota(jnp.int32, scores.shape, 1)
    scores = jnp.where((rows >= cols) & (segc == segr), scores, -1e30)
    grown = jnp.exp(scores - jnp.max(scores, axis=-1, keepdims=True))
    return grown / jnp.sum(grown, axis=-1, keepdims=True)


def attention_forward_kernel(q_ref, k_ref, v_ref, segc_ref, segr_ref, o_ref):
    probs = attention_probs(q_ref[...], k_ref[...], segc_ref[...], segr_ref[...], pl.program_id(1))
    o_ref[...] = mm(probs.astype(BF16), v_ref[...]).astype(BF16)


def attention_backward_kernel(
    q_ref, k_ref, v_ref, segc_ref, segr_ref, g_ref, dq_ref, dk_ref, dv_ref
):
    @pl.when((pl.program_id(0) == 0) & (pl.program_id(1) == 0))
    def _():
        dk_ref[...] = jnp.zeros_like(dk_ref)
        dv_ref[...] = jnp.zeros_like(dv_ref)

    q, k, g = q_ref[...], k_ref[...], g_ref[...]
    probs = attention_probs(q, k, segc_ref[...], segr_ref[...], pl.program_id(1))
    d_probs = mm_nt(g, v_ref[...])
    inner = jnp.sum(probs * d_probs, axis=-1, keepdims=True)
    d_scores = (probs * (d_probs - inner)).astype(BF16)
    dq_ref[...] = mm(d_scores, k) * SCALE
    dk_ref[...] += mm_tn(d_scores, q) * SCALE
    dv_ref[...] += mm_tn(probs.astype(BF16), g)


def attention_specs(tokens):
    block = pl.BlockSpec((Q_BLOCK, HEAD_SIZE), lambda h, i: (i, h))
    whole = pl.BlockSpec((tokens, HEAD_SIZE), lambda h, i: (0, 0))
    segc = pl.BlockSpec((Q_BLOCK, 1), lambda h, i: (i, 0))
    segr = pl.BlockSpec((1, tokens), lambda h, i: (0, 0))
    params = pltpu.CompilerParams(
        dimension_semantics=("arbitrary", "arbitrary"), vmem_limit_bytes=32 << 20
    )
    return block, whole, segc, segr, params


def attention_forward(q, k, v, segc, segr):
    tokens = q.shape[0]
    block, whole, sc, sr, params = attention_specs(tokens)
    return pl.pallas_call(
        attention_forward_kernel,
        grid=(QH, tokens // Q_BLOCK),
        in_specs=[block, whole, whole, sc, sr],
        out_specs=block,
        out_shape=jax.ShapeDtypeStruct((tokens, QH * HEAD_SIZE), BF16),
        compiler_params=params,
        name="attention_forward",
    )(q, k, v, segc, segr)


def attention_backward(q, k, v, segc, segr, g):
    tokens = q.shape[0]
    block, whole, sc, sr, params = attention_specs(tokens)
    return pl.pallas_call(
        attention_backward_kernel,
        grid=(QH, tokens // Q_BLOCK),
        in_specs=[block, whole, whole, sc, sr, block],
        out_specs=[block, whole, whole],
        out_shape=[
            jax.ShapeDtypeStruct((tokens, QH * HEAD_SIZE), F32),
            jax.ShapeDtypeStruct((tokens, HEAD_SIZE), F32),
            jax.ShapeDtypeStruct((tokens, HEAD_SIZE), F32),
        ],
        compiler_params=params,
        name="attention_backward",
    )(q, k, v, segc, segr, g)


def rms_of(rows):
    return lax.rsqrt(jnp.mean(rows * rows, axis=-1, keepdims=True) + NORM_EPSILON)


def norm_back(grad, rows, r, gain):
    w = grad * gain
    return r * w - rows * (r * r * r) * jnp.mean(w * rows, axis=-1, keepdims=True)


def silu_slope(value):
    sg = jax.nn.sigmoid(value)
    return sg * (1.0 + value * (1.0 - sg))


def turned(heads, cosine, sine):
    half = HEAD_SIZE // 2
    parts = []
    for h in range(heads.shape[1] // HEAD_SIZE):
        v = heads[:, h * HEAD_SIZE : (h + 1) * HEAD_SIZE]
        parts.append(v * cosine + jnp.concatenate([v[:, half:], v[:, :half]], axis=1) * sine)
    return jnp.concatenate(parts, axis=1)


def shifted(value, lag):
    if lag == 0:
        return value
    zeros = jnp.zeros((abs(lag), value.shape[1]), value.dtype)
    if lag > 0:
        return jnp.concatenate([zeros, value[:-lag]], axis=0)
    return jnp.concatenate([value[-lag:], zeros], axis=0)


def convolve(value, taps, keeps):
    total = taps[0][None] * value
    for lag in range(1, TAPS):
        total = total + taps[lag][None] * shifted(value, lag) * keeps[lag]
    return total


def body(
    tokens,
    segment_ids,
    valid_mask,
    teacher,
    mixer_in,
    mixer_out,
    query_weight,
    key_value_weight,
    output_weight,
    gate_up,
    down_weight,
    norm_first,
    norm_second,
    conv_taps,
    decay_log,
    skip_gain,
    step_bias,
):
    ring = Ring()
    nb = ring.n
    j = lax.axis_index("ctx")
    own = tokens.shape[0] * tokens.shape[1]
    length = own * NC
    devices = nb * NC
    total_tokens = float(own * devices)
    x = tokens.reshape(own, MODEL_WIDTH).astype(F32)
    valid = valid_mask.reshape(own).astype(F32)
    target = teacher.reshape(own, MODEL_WIDTH).astype(F32)

    order = Order(jnp.broadcast_to(valid[:1] * 0.0, (8, 128)))
    gate, scale = order.gate, max(1, nb // 8)

    def turn(run, *others):
        for _ in range(scale):
            if not run.over:
                others = run.turn(others)
        return others[0] if len(others) == 1 else others

    def finish(run, *others):
        while not run.over:
            others = run.turn(others)
        return others[0] if len(others) == 1 else others

    def start(block, place=lambda b: b):
        return GatherRun(ring, order, block, place)

    rows = mixer_in.shape[0]
    edge = 2 * DI + 2 * N
    unit = down_weight.shape[0]
    down_half = MODEL_WIDTH // 2
    g_da = start(down_weight[:, :down_half])

    xs_cols = mixer_in[:, DI : 2 * DI].reshape(rows, NC, WX)
    bc_cols = mixer_in[:, 2 * DI : edge].reshape(rows, NC, WB)
    dt_cols = jnp.pad(mixer_in[:, edge:].reshape(rows, NC, HEADS), ((0, 0), (0, 0), (0, 128 - HEADS)))
    first_cols = jnp.concatenate([xs_cols, bc_cols, dt_cols], axis=2).transpose(1, 0, 2)
    spread = Spread(first_cols, j)
    spread.got, mixer_in, query_weight, key_value_weight, x = turn(
        g_da, spread.got, mixer_in, query_weight, key_value_weight, x
    )
    spread.cross()
    z_cols = mixer_in[:, :DI].reshape(rows, NC, WX)
    q_cols = query_weight.reshape(rows, NC, WQ)
    kv = key_value_weight.reshape(rows, 2, 2, HEAD_SIZE)
    kv_cols = kv.transpose(0, 2, 1, 3).reshape(rows, NC, HEAD_SIZE)
    second_cols = jnp.concatenate([q_cols, kv_cols, z_cols], axis=2).transpose(1, 0, 2)
    spread_two = Spread(second_cols, j)
    r_x = rms_of(x)
    normed_own = (x * r_x * norm_first).astype(BF16)
    spread.across, segment_ids, valid, normed_own = turn(
        g_da, spread.across, segment_ids, valid, normed_own
    )
    g_first = start(spread.block())
    near_normed = Near(normed_own)
    near_seg = Near(segment_ids.reshape(1, own))
    count = sum_everywhere(jnp.broadcast_to(jnp.sum(valid), (1, 128)), nb)
    near_seg.far, near_seg.next, spread_two.got = turn(
        g_da, near_seg.far, near_seg.next, spread_two.got
    )
    near_seg.cross()
    spread_two.cross()
    mixer_out, output_weight, gate_up = finish(g_da, mixer_out, output_weight, gate_up)
    rows_out, rows_attn = mixer_out.shape[0], output_weight.shape[0]

    def home(q):
        return (q % 2) * 4 + q // 2 % 2 * 2 + q // 4 if nb == 8 else q

    there = [(m, home(m % nb) * NC + m // nb) for m in range(devices)]
    back = [(b, a) for a, b in there]
    both_out = lax.ppermute(
        jnp.concatenate([mixer_out, output_weight], axis=0), ("batch", "ctx"), there
    )
    near_normed.far, near_normed.next, spread_two.across, near_seg.last = turn(
        g_first, near_normed.far, near_normed.next, spread_two.across, near_seg.last
    )
    near_normed.cross()
    gu_cols = (
        gate_up.reshape(rows, 2, nb, NC, unit).transpose(3, 0, 1, 2, 4).reshape(NC, rows, 2 * WF)
    )
    spread_gu = Spread(gu_cols, j)
    near_normed.last, count = turn(g_first, near_normed.last, count)
    g_second = start(spread_two.block())
    normed = absolute(near_normed.blocks(), j).reshape(length, MODEL_WIDTH)
    spread_gu.got, normed = turn(g_first, spread_gu.got, normed)
    spread_gu.cross()

    seg = absolute(near_seg.blocks(), j).reshape(length)
    keeps = [None]
    for lag in range(1, TAPS):
        before = jnp.concatenate([jnp.full((lag,), -1, jnp.int32), seg[:-lag]])
        keeps.append((before == seg).astype(F32)[:, None])
    place = jnp.arange(length, dtype=jnp.int32)
    half = HEAD_SIZE // 2
    inverse = ROPE_BASE ** (-(jnp.arange(half, dtype=F32) * 2.0) / HEAD_SIZE)
    angle = place.astype(F32)[:, None] * inverse[None, :]
    cosine, sine = jnp.cos(angle), jnp.sin(angle)
    cosine = jnp.concatenate([cosine, cosine], axis=1)
    sine = jnp.concatenate([-sine, sine], axis=1)
    heads_at = j * HEADS
    own_log = lax.dynamic_slice_in_dim(decay_log, heads_at, HEADS)
    own_bias = lax.dynamic_slice_in_dim(step_bias, heads_at, HEADS)
    own_skip = lax.dynamic_slice_in_dim(skip_gain, heads_at, HEADS)
    skip_wide = jnp.repeat(own_skip, P_SIZE)[None, :]
    taps_x = lax.dynamic_slice(conv_taps, (0, j * WX), (TAPS, WX))
    taps_b = conv_taps[:, DI:]
    taps_b_own = lax.dynamic_slice(conv_taps, (0, DI + j * WB), (TAPS, WB))
    cosine, sine, seg, normed, spread_gu.across = finish(
        g_first, cosine, sine, seg, normed, spread_gu.across
    )
    w_first = g_first.whole

    conv_b_own = mm(normed, w_first[:, WX : WX + WB]).astype(BF16)
    b_far = y_swap(conv_b_own)
    conv_b_own, normed, w_first = turn(g_second, conv_b_own, normed, w_first)
    step_raw = mm(normed, w_first[:, WX + WB :])[:, :HEADS]
    conv_x = mm(normed, w_first[:, :WX]).astype(BF16)
    conv_x, step_raw, b_far, both_out = turn(g_second, conv_x, step_raw, b_far, both_out)
    b_other = core_swap(jnp.concatenate([conv_b_own, b_far], axis=1))
    g_out = start(both_out, lambda b: home(b))
    upper, core = j // 2, j % 2
    mine = (jnp.where(upper == 0, conv_b_own, b_far), jnp.where(upper == 0, b_far, conv_b_own))
    theirs = (
        jnp.where(upper == 0, b_other[:, :WB], b_other[:, WB:]),
        jnp.where(upper == 0, b_other[:, WB:], b_other[:, :WB]),
    )
    conv_b = jnp.concatenate(
        [
            jnp.where(core == 0, mine[0], theirs[0]),
            jnp.where(core == 0, theirs[0], mine[0]),
            jnp.where(core == 0, mine[1], theirs[1]),
            jnp.where(core == 0, theirs[1], mine[1]),
        ],
        axis=1,
    )
    conv_out_x = convolve(conv_x.astype(F32), taps_x, keeps)
    xs = jax.nn.silu(conv_out_x)
    xs, conv_out_x, conv_b, step_raw = turn(g_second, xs, conv_out_x, conv_b, step_raw)
    bc = jax.nn.silu(convolve(conv_b.astype(F32), taps_b, keeps))
    bmat, cmat = bc[:, :N], bc[:, N:]

    step_in = step_raw + own_bias
    step = jax.nn.softplus(step_in)
    rate = jnp.exp(own_log)
    decay = -rate * step
    chunks = length // CHUNK
    lower = jnp.tril(jnp.ones((CHUNK, CHUNK), F32))
    by_chunk = decay.reshape(chunks, CHUNK, HEADS)
    cum = jnp.einsum("ts,csh->cth", lower, by_chunk, precision=HIGHEST)
    seg_c = seg.reshape(chunks, CHUNK)
    seg_last = seg_c[:, -1]
    seg_prev = jnp.concatenate([jnp.full((1,), -1, jnp.int32), seg_last[:-1]])
    reach = jnp.exp(cum) * (seg_c == seg_prev[:, None]).astype(F32)[:, :, None]
    bare = jnp.exp(cum[:, -1:, :] - cum) * (seg_c == seg_last[:, None]).astype(F32)[:, :, None]
    weight = bare * step.reshape(chunks, CHUNK, HEADS)
    through = jnp.exp(cum[:, -1]) * (seg_last == seg_prev).astype(F32)[:, None]
    seg_f = seg.astype(F32)
    colv = jnp.concatenate(
        [
            cum.reshape(length, HEADS),
            reach.reshape(length, HEADS),
            weight.reshape(length, HEADS),
            bare.reshape(length, HEADS),
            seg_f[:, None],
            jnp.zeros((length, 128 - 4 * HEADS - 1), F32),
        ],
        axis=1,
    )
    rowv = jnp.concatenate(
        [
            cum.reshape(length, HEADS).T,
            step.T,
            seg_f[None, :],
            jnp.zeros((32 - 2 * HEADS - 1, length), F32),
        ],
        axis=0,
    )
    bmat, cmat, colv, rowv, xs = finish(g_second, bmat, cmat, colv, rowv, xs)
    w_second = g_second.whole
    bmat, cmat, colv, rowv, xs = turn(g_out, bmat, cmat, colv, rowv, xs)
    ssm_y, states = ssd_forward(through, xs, bmat, cmat, colv, rowv, skip_wide)
    ssm_y, normed = turn(g_out, ssm_y, normed)
    rest = mm(normed, w_second)
    rest = turn(g_out, rest)
    g_gu = start(spread_gu.block())
    gate_z = rest[:, WQ + HEAD_SIZE :]
    queries = turned(rest[:, :WQ], cosine, sine).astype(BF16)
    kv_raw = rest[:, WQ : WQ + HEAD_SIZE]
    kv_own = jnp.where(core == 0, turned(kv_raw, cosine, sine), kv_raw).astype(BF16)
    kv_other = core_swap(kv_own)
    keys = jnp.where(core == 0, kv_own, kv_other)
    values = jnp.where(core == 0, kv_other, kv_own)
    segc, segr = seg[:, None], seg[None, :]
    attended = attention_forward(queries, keys, values, segc, segr)
    silu_z = jax.nn.silu(gate_z)
    gated = (ssm_y * silu_z).astype(BF16)
    acts = jnp.concatenate([gated, attended], axis=1)
    acts = finish(g_out, acts)
    out_all = g_out.whole.reshape(nb, rows_out + rows_attn, MODEL_WIDTH)
    w_out = jnp.concatenate(
        [
            out_all[:, :rows_out].reshape(WX, MODEL_WIDTH),
            out_all[:, rows_out:].reshape(WQ, MODEL_WIDTH),
        ],
        axis=0,
    )

    mixed = NearSum(lambda k: mm(lax.dynamic_slice_in_dim(acts, (j ^ k) * own, own), w_out))
    mixed.first, mixed.near = turn(g_gu, mixed.first, mixed.near)
    (mixed.second,) = gate(mixed.second)
    hidden_one = x + mixed.result()
    r_h = rms_of(hidden_one)
    normed_two_own = (hidden_one * r_h * norm_second).astype(BF16)
    (normed_two_own,) = gate(normed_two_own)
    near_two = Near(normed_two_own)
    near_two.next, down_b = turn(g_gu, near_two.next, down_weight[:, down_half:])
    (near_two.far,) = gate(near_two.far)
    near_two.cross()
    g_db = start(down_b)
    near_two.last = turn(g_gu, near_two.last)
    normed_two = near_two.blocks()
    normed_two_all = stacked(normed_two)
    normed_two = list(finish(g_gu, *normed_two))
    w_gu = g_gu.whole

    gates = []
    hidden_all = jnp.zeros((length, WF), BF16)
    for k in range(NC):
        gateup = mm(normed_two[k], w_gu)
        gateup = turn(g_db, gateup)
        gates.append(gateup)
        piece = (jax.nn.silu(gateup[:, :WF]) * gateup[:, WF:]).astype(BF16)
        hidden_all = lax.dynamic_update_slice(hidden_all, piece, (k * own, 0))

    def near_rows(value, k):
        return value[k * own : (k + 1) * own]

    hidden_all = finish(g_db, hidden_all)
    count = count[0, 0]
    w_down = jnp.concatenate([g_da.whole, g_db.whole], axis=1)
    ffn = NearSum(lambda k: mm(near_rows(hidden_all, k), w_down))
    (ffn.second,) = gate(ffn.second)
    final = hidden_one + ffn.result()
    error = final - target
    squares = jnp.sum(valid * jnp.sum(error * error, axis=1))
    grad_final = valid[:, None] * error * (total_tokens / count)
    grad_ffn_own = grad_final.astype(BF16)

    def block_of(left, size, right):
        def part(slot):
            return mm_tn(
                lax.dynamic_slice_in_dim(left, ring.owner(slot) * size, size, axis=1), right
            )

        return part

    def reduce(part):
        return ReduceRun(ring, order, part)

    (grad_ffn_own,) = gate(grad_ffn_own)
    near_ffn = Near(grad_ffn_own)
    d_gateup_all = jnp.zeros((length, 2 * WF), BF16)

    def ffn_back(whole, grad, k):
        d_hidden = mm_nt(grad, w_down)
        gate_k, up_k = gates[k][:, :WF], gates[k][:, WF:]
        d_gate = (d_hidden * up_k * silu_slope(gate_k)).astype(BF16)
        d_up = (d_hidden * jax.nn.silu(gate_k)).astype(BF16)
        whole = lax.dynamic_update_slice(whole, d_gate, (k * own, 0))
        return lax.dynamic_update_slice(whole, d_up, (k * own, WF))

    d_gateup_all = ffn_back(d_gateup_all, near_ffn.own, 0)
    d_gateup_all = ffn_back(d_gateup_all, near_ffn.next, 1)
    near_ffn.far, near_ffn.next, d_gateup_all = gate(near_ffn.far, near_ffn.next, d_gateup_all)
    near_ffn.cross()
    d_gateup_all = ffn_back(d_gateup_all, near_ffn.far, 2)
    grad_ffn_all = stacked(near_ffn.blocks())
    r_down = reduce(block_of(hidden_all, unit, grad_ffn_all))
    d_gateup_all = ffn_back(d_gateup_all, near_ffn.last, 3)
    two = NearSum(lambda k: mm_nt(near_rows(d_gateup_all, k), w_gu))
    r_gu = reduce(block_of(normed_two_all, NC * rows, d_gateup_all))
    two.first, two.near = turn(r_down, two.first, two.near)
    two.near = turn(r_down, two.near)
    two.near = turn(r_gu, two.near)
    two.second, two.near = gate(two.second, two.near)
    grad_normed_two = two.result()
    w_two = norm_back(grad_normed_two, hidden_one, r_h, norm_second)
    g_norm_second = jnp.sum(grad_normed_two * hidden_one * r_h, axis=0)
    grad_hidden_one = grad_final + w_two
    branch_own = grad_hidden_one.astype(BF16)
    branch_own, grad_hidden_one, g_norm_second = gate(branch_own, grad_hidden_one, g_norm_second)
    near_branch = Near(branch_own)
    near_branch.next = turn(r_down, near_branch.next)
    near_branch.next = turn(r_gu, near_branch.next)
    near_branch.next = finish(r_down, near_branch.next)
    (near_branch.far,) = gate(near_branch.far)
    near_branch.cross()
    near_branch.last = turn(r_gu, near_branch.last)
    branch = absolute(near_branch.blocks(), j).reshape(length, MODEL_WIDTH)
    d_acts = mm_nt(branch, w_out)
    grad_attended = d_acts[:, WX:].astype(BF16)
    grad_gated = d_acts[:, :WX]
    grad_ssm_y = grad_gated * silu_z
    d_z = (grad_gated * ssm_y * silu_slope(gate_z)).astype(BF16)
    grad_attended, grad_ssm_y, d_z, branch = gate(grad_attended, grad_ssm_y, d_z, branch)

    def out_part(slot):
        b = home(ring.owner(slot))
        left = jnp.concatenate(
            [
                lax.dynamic_slice_in_dim(gated, b * rows_out, rows_out, axis=1),
                lax.dynamic_slice_in_dim(attended, b * rows_attn, rows_attn, axis=1),
            ],
            axis=1,
        )
        return mm_tn(left, branch)

    r_out = reduce(out_part)

    grad_attended = finish(r_gu, grad_attended)
    dq, dk, dv = attention_backward(queries, keys, values, segc, segr, grad_attended)
    sent = jnp.where(core == 0, dv, dk)
    d_kv_other = core_swap(sent)
    dq, dk, dv, d_kv_other = turn(r_out, dq, dk, dv, d_kv_other)
    d_query = turned(dq, cosine, -sine).astype(BF16)
    d_kv = jnp.where(core == 0, dk, dv) + d_kv_other
    d_kv = jnp.where(core == 0, turned(d_kv, cosine, -sine), d_kv).astype(BF16)
    d_second = jnp.concatenate([d_query, d_kv, d_z], axis=1)
    r_second = reduce(block_of(normed, NC * rows, d_second))

    def collected(run):
        return Collect(run.result.astype(BF16).reshape(NC, rows, run.result.shape[1]), j)

    grad_ssm_y, d_second = turn(r_out, grad_ssm_y, d_second)
    operands = (grad_ssm_y, xs, bmat, cmat, colv, rowv, skip_wide, states)
    dx, dbc, dcol, drow_a = ssd_backward(0, through, *operands)
    col_gu = collected(r_gu)
    dx, dbc, dcol, col_gu.got = turn(r_second, dx, dbc, dcol, col_gu.got)
    col_gu.cross()
    dx, dbc, dcol = turn(r_out, dx, dbc, dcol)
    dx, dbc, dcol, drow_b = ssd_backward(1, through, *operands, (dbc, dcol, dx))
    drow = jnp.concatenate([drow_a[: HEADS // 2], drow_b[: HEADS // 2]], axis=0)
    dx, dbc, dcol, drow = turn(r_second, dx, dbc, dcol, drow)
    dx, dbc, dcol, drow = finish(r_out, dx, dbc, dcol, drow)
    b_sum = NearSum(lambda k: lax.dynamic_index_in_dim(dbc, j ^ k, 0, False))
    g_skip = jnp.sum(jnp.sum(grad_ssm_y * xs, axis=0).reshape(HEADS, P_SIZE), axis=1)
    drow_t = drow.T
    d_cum = dcol[:, :HEADS] - step * drow_t
    d_decay = jnp.einsum(
        "ts,cth->csh", lower, d_cum.reshape(chunks, CHUNK, HEADS), precision=HIGHEST
    ).reshape(length, HEADS)
    d_step = dcol[:, HEADS : 2 * HEADS] + drow_t - rate * d_decay
    d_raw = d_step * jax.nn.sigmoid(step_in)
    g_bias = jnp.sum(d_raw, axis=0)
    g_log = jnp.sum(d_decay * decay, axis=0)

    def conv_back(d_conv, value, taps):
        d_in = taps[0][None] * d_conv
        g_taps = [jnp.sum(d_conv * value, axis=0)]
        for lag in range(1, TAPS):
            masked = d_conv * keeps[lag]
            d_in = d_in + taps[lag][None] * shifted(masked, -lag)
            g_taps.append(jnp.sum(masked * shifted(value, lag), axis=0))
        return d_in.astype(BF16), jnp.stack(g_taps)

    d_in_x, g_taps_x = conv_back(dx * silu_slope(conv_out_x), conv_x.astype(F32), taps_x)
    d_in_x, b_sum.second, b_sum.near, b_sum.first = turn(
        r_second, d_in_x, b_sum.second, b_sum.near, b_sum.first
    )
    conv_b_wide = conv_b_own.astype(F32)
    conv_out_b = convolve(conv_b_wide, taps_b_own, keeps)
    d_in_b, g_taps_b = conv_back(b_sum.result() * silu_slope(conv_out_b), conv_b_wide, taps_b_own)
    d_first = jnp.concatenate(
        [d_in_x, d_in_b, jnp.pad(d_raw.astype(BF16), ((0, 0), (0, 128 - HEADS)))], axis=1
    )
    r_first = reduce(block_of(normed, NC * rows, d_first))
    d_first, d_second = finish(r_second, d_first, d_second)

    def normed_part(k):
        at = (j ^ k) * own
        return mm_nt(lax.dynamic_slice_in_dim(d_first, at, own), w_first) + mm_nt(
            lax.dynamic_slice_in_dim(d_second, at, own), w_second
        )

    back_sum = NearSum(normed_part)
    col_second = collected(r_second)
    back_sum.near, col_second.got = turn(r_first, back_sum.near, col_second.got)
    col_second.cross()
    out_home = lax.ppermute(r_out.result.astype(BF16), ("batch", "ctx"), back).astype(F32)
    back_sum.near = turn(r_first, back_sum.near)
    back_sum.second, back_sum.near = turn(r_first, back_sum.second, back_sum.near)
    grad_normed = back_sum.result()
    g_norm_first = jnp.sum(grad_normed * x * r_x, axis=0)
    grad_tokens = grad_hidden_one + norm_back(grad_normed, x, r_x, norm_first)
    g_norm_first = finish(r_first, g_norm_first)
    col_first = collected(r_first)

    taps_all = jnp.zeros((TAPS, DI + 2 * N), F32)
    taps_all = lax.dynamic_update_slice(taps_all, g_taps_x, (0, j * WX))
    taps_all = lax.dynamic_update_slice(taps_all, g_taps_b, (0, DI + j * WB))
    per_head = lax.dynamic_update_slice(
        jnp.zeros((3, 128), F32), jnp.stack([g_log, g_skip, g_bias]), (0, heads_at)
    )
    small = sum_everywhere(
        jnp.concatenate(
            [
                g_norm_first.reshape(-1, 128),
                g_norm_second.reshape(-1, 128),
                taps_all.reshape(-1, 128),
                per_head,
                jnp.broadcast_to(squares, (1, 128)),
            ]
        ),
        nb,
    )
    lines = MODEL_WIDTH // 128
    g_norm_first = small[:lines].reshape(MODEL_WIDTH)
    g_norm_second = small[lines : 2 * lines].reshape(MODEL_WIDTH)
    taps_all = small[2 * lines : -4].reshape(TAPS, DI + 2 * N)
    per_head = small[-4:-1, :H_M]
    loss_value = small[-1, 0] / (MODEL_WIDTH * count) + order.token[0, 0]
    col_first.cross()

    got_gu = col_gu.result()
    grad_gate_up = (
        got_gu.reshape(NC, rows, 2, nb, unit).transpose(1, 2, 3, 0, 4).reshape(rows, 2 * FF)
    )
    got_second = col_second.result()
    got_first = col_first.result()

    def columns(got, begin, size):
        return got[:, :, begin : begin + size].transpose(1, 0, 2).reshape(rows, NC * size)

    grad_query = columns(got_second, 0, WQ)
    grad_keyval = (
        got_second[:, :, WQ : WQ + HEAD_SIZE]
        .reshape(2, 2, rows, HEAD_SIZE)
        .transpose(2, 1, 0, 3)
        .reshape(rows, 4 * HEAD_SIZE)
    )
    grad_mixer_in = jnp.concatenate(
        [
            columns(got_second, WQ + HEAD_SIZE, WX),
            columns(got_first, 0, WX),
            columns(got_first, WX, WB),
            columns(got_first, WX + WB, HEADS),
        ],
        axis=1,
    )
    output = final.astype(BF16).reshape(tokens.shape)
    return (
        output,
        loss_value,
        grad_tokens.reshape(tokens.shape),
        grad_mixer_in,
        out_home[:rows_out],
        grad_query,
        grad_keyval,
        out_home[rows_out:],
        grad_gate_up,
        r_down.result,
        g_norm_first,
        g_norm_second,
        taps_all,
        per_head[0],
        per_head[1],
        per_head[2],
    )


def solution(mesh):
    split_rows = P(("batch", "ctx"), None)
    by_token = P("batch", "ctx", None)
    return jax.shard_map(
        body,
        mesh=mesh,
        in_specs=(by_token, P("batch", "ctx"), P("batch", "ctx"), by_token)
        + (split_rows,) * 7
        + (P(),) * 6,
        out_specs=(by_token, P(), by_token) + (split_rows,) * 7 + (P(),) * 6,
        check_vma=False,
    )
```

```python
import functools

import jax
import jax.numpy as jnp
from jax import lax
from jax.experimental import pallas as pl
from jax.experimental.pallas import tpu as pltpu
from jax.sharding import PartitionSpec as P

MODEL_WIDTH = 2048
H_M = 48
P_SIZE = 64
N = 256
QUERY_HEADS = 8
KEY_VALUE_HEADS = 2
HEAD_SIZE = 128
FF = 4096
TAPS = 4
DI = 3072

NC = 4
HEADS = H_M // NC
PAIRS = HEADS // 2
WX = DI // NC
WB = 2 * N // NC
WQ = QUERY_HEADS * HEAD_SIZE // NC
QH = QUERY_HEADS // NC
WF = FF // NC
CHUNK = 128

NORM_EPSILON = 1e-05
ROPE_BASE = 1000000.0
HIGHEST = lax.Precision.HIGHEST
F32 = jnp.float32
BF16 = jnp.bfloat16


def mm(left, right):
    return jnp.dot(left, right, preferred_element_type=F32)


def mm_tn(left, right):
    return lax.dot_general(left, right, (((0,), (0,)), ((), ())), preferred_element_type=F32)


def mm_nt(left, right):
    return lax.dot_general(left, right, (((1,), (1,)), ((), ())), preferred_element_type=F32)


def after(value, *deps):
    return lax.optimization_barrier((value,) + deps)[0]


def core_swap(value):
    return lax.ppermute(value, "ctx", [(i, i ^ 1) for i in range(NC)])


def y_swap(value):
    return lax.ppermute(value, "ctx", [(i, i ^ 2) for i in range(NC)])


class Ring:
    def __init__(self):
        self.n = lax.axis_size("batch")
        n = self.n
        order = list(range(0, n, 2)) + list(range(n - 1, 0, -2))
        self.up_pairs = [(order[i], order[(i + 1) % n]) for i in range(n)]
        self.down_pairs = [(order[(i + 1) % n], order[i]) for i in range(n)]
        b = lax.axis_index("batch")
        self.pos = jnp.where(b % 2 == 0, b // 2, n - 1 - b // 2)

    def up(self, value):
        return lax.ppermute(value, "batch", self.up_pairs)

    def down(self, value):
        return lax.ppermute(value, "batch", self.down_pairs)

    def owner(self, slot):
        p = (self.pos + slot + self.n) % self.n
        return jnp.where(p < self.n // 2, 2 * p, 2 * (self.n - 1 - p) + 1)


class Order:
    def __init__(self, token):
        self.token = token

    def gate(self, *values):
        out = lax.optimization_barrier(values + (self.token,))
        self.token = out[-1]
        return out[:-1]


class GatherRun:
    def __init__(self, ring, order, block, place=lambda b: b):
        self.ring, self.order, self.place = ring, order, place
        self.rows, cols = block.shape
        (block,) = order.gate(block)
        self.down, self.up = ring.down(block), ring.up(block)
        self.whole = jnp.zeros((ring.n * self.rows, cols), block.dtype)
        self.put(block, 0)
        self.step, self.over = 1, False

    def put(self, part, slot, offset=0):
        at = self.place(self.ring.owner(slot)) * self.rows + offset
        self.whole = lax.dynamic_update_slice(self.whole, part, (at, 0))

    def turn(self, others):
        ring, far, half = self.ring, self.ring.n // 2, self.rows // 2
        down, up, *others = self.order.gate(self.down, self.up, *others)
        if self.step < far:
            if self.step + 1 < far:
                self.down, self.up = ring.down(down), ring.up(up)
            else:
                self.down, self.up = ring.down(down[half:]), ring.up(up[:half])
            self.put(down, self.step)
            self.put(up, -self.step)
        else:
            self.put(up, far)
            self.put(down, far, half)
            self.over = True
        self.step += 1
        return others


class ReduceRun:
    def __init__(self, ring, order, part):
        self.ring, self.order, self.part = ring, order, part
        far = part(ring.n // 2)
        (far,) = order.gate(far)
        self.half = far.shape[0] // 2
        self.up, self.down = ring.up(far[: self.half]), ring.down(far[self.half :])
        self.step, self.over = ring.n // 2 - 1, False

    def turn(self, others):
        half = self.half
        up, down, *others = self.order.gate(self.up, self.down, *others)
        up, down = up.astype(F32), down.astype(F32)
        if self.step == 0:
            self.result = self.part(0).astype(F32) + up + down
            self.over = True
            return others
        a, b = self.part(self.step), self.part(-self.step)
        if self.step == self.ring.n // 2 - 1:
            a = lax.dynamic_update_slice(a, (a[:half].astype(F32) + up).astype(BF16), (0, 0))
            b = lax.dynamic_update_slice(b, (b[half:].astype(F32) + down).astype(BF16), (half, 0))
        else:
            a = (a.astype(F32) + up).astype(BF16)
            b = (b.astype(F32) + down).astype(BF16)
        self.up, self.down = self.ring.up(a), self.ring.down(b)
        self.step -= 1
        return others


def sum_everywhere(value, batch):
    value = value + core_swap(value)
    value = value + y_swap(value)
    bit = 1
    while bit < batch:
        value = value + lax.ppermute(value, "batch", [(i, i ^ bit) for i in range(batch)])
        bit *= 2
    return value


class Spread:
    def __init__(self, parts, j):
        self.parts, self.j = parts, j
        self.got = y_swap(jnp.stack([parts[j ^ 2], parts[j ^ 3]]))

    def cross(self):
        self.across = core_swap(jnp.stack([self.parts[self.j ^ 1], self.got[1]]))

    def block(self):
        blocks = [self.parts[self.j], self.across[0], self.got[0], self.across[1]]
        whole = absolute(blocks, self.j)
        return whole.reshape(NC * whole.shape[1], whole.shape[2])


class Collect:
    def __init__(self, block, j):
        self.block, self.j = block, j
        self.got = core_swap(jnp.stack([block[j ^ 1], block[j ^ 3]]))

    def cross(self):
        self.far = y_swap(jnp.stack([self.block[self.j ^ 2], self.got[1]]))

    def result(self):
        whole = absolute([self.block[self.j], self.got[0], self.far[0], self.far[1]], self.j)
        return whole.astype(F32)


def absolute(blocks, j):
    whole = jnp.zeros((NC,) + blocks[0].shape, blocks[0].dtype)
    for k in range(NC):
        whole = lax.dynamic_update_slice(
            whole, blocks[k][None], (j ^ k,) + (0,) * blocks[0].ndim
        )
    return whole


def stacked(blocks):
    size = blocks[0].shape[0]
    whole = jnp.zeros((len(blocks) * size,) + blocks[0].shape[1:], blocks[0].dtype)
    for k, block in enumerate(blocks):
        whole = lax.dynamic_update_slice_in_dim(whole, block, k * size, 0)
    return whole


class Near:
    def __init__(self, own):
        self.own, self.far, self.next = own, y_swap(own), core_swap(own)

    def cross(self):
        self.last = core_swap(self.far)

    def blocks(self):
        return [self.own, self.next, self.far, self.last]


class NearSum:
    def __init__(self, part, at, between=None):
        self.part, self.at = part, at
        self.away = part(True)
        self.third = core_swap(self.away[1 - at].astype(BF16))
        if between is None:
            self.go()
            self.stay()

    def go(self):
        self.second = y_swap((self.away[self.at] + self.third.astype(F32)).astype(BF16))

    def stay(self):
        home = self.part(False)
        self.first = core_swap(home[1 - self.at].astype(BF16))
        self.near = home[self.at]

    def result(self):
        return self.near + self.first.astype(F32) + self.second.astype(F32)


PAIR = 2 * P_SIZE
EDGE = 8


def halves(first, second, lanes):
    return jnp.where(lanes < P_SIZE, first, second)


def step_values(raw, bias, log, marks):
    rows = lax.broadcasted_iota(jnp.int32, (CHUNK, CHUNK), 0)
    cols = lax.broadcasted_iota(jnp.int32, (CHUNK, CHUNK), 1)
    value = raw + bias
    step = jnp.maximum(value, 0.0) + jnp.log1p(jnp.exp(-jnp.abs(value)))
    decay = -jnp.exp(log) * step
    lower = (rows >= cols).astype(F32)
    cum = jnp.dot(lower, decay, precision=HIGHEST, preferred_element_type=F32)
    end = cum[CHUNK - 1 :, :]
    seg, before, last = marks[:, 0:1], marks[:, 1:2], marks[:, 2:3]
    reach = jnp.where(seg == before, jnp.exp(cum), 0.0)
    bare = jnp.where(seg == last, jnp.exp(end - cum), 0.0)
    through = jnp.where(last[:1] == before[:1], jnp.exp(end), 0.0)
    return value, step, decay, cum, reach, bare, through


def convolved(buf, taps, marks, width):
    total = taps[0:1, :width] * buf[EDGE : EDGE + CHUNK, :width]
    for lag in range(1, TAPS):
        moved = buf[EDGE - lag : EDGE - lag + CHUNK, :width]
        total = total + taps[lag : lag + 1, :width] * moved * marks[:, 2 + lag : 3 + lag]
    return total


def ssd_forward_kernel(
    x_ref, bc_ref, raw_ref, bias_ref, log_ref, taps_ref, tapsb_ref, mark_ref, row_ref, skip_ref,
    y_ref, st_ref, conv_ref, act_ref, step_ref, reach_ref, bare_ref, cum_ref, cumt_ref, end_ref,
    state, buf, bufb
):
    @pl.when(pl.program_id(0) == 0)
    def _():
        state[...] = jnp.zeros_like(state)
        buf[...] = jnp.zeros_like(buf)
        bufb[...] = jnp.zeros_like(bufb)

    marks = mark_ref[...]
    for b_, ref in ((buf, x_ref), (bufb, bc_ref)):
        b_[0:EDGE, :] = b_[CHUNK : CHUNK + EDGE, :]
        b_[EDGE : EDGE + CHUNK, :] = ref[...].astype(F32)
    conv = convolved(bufb, tapsb_ref, marks, 2 * N)
    bc = (conv * jax.nn.sigmoid(conv)).astype(BF16)
    act_ref[...] = bc
    b, c = bc[:, :N], bc[:, N:]
    _, step, _, cum, reach, bare, through = step_values(
        raw_ref[...], bias_ref[...], log_ref[...], marks
    )
    weight = bare * step
    cum_rows = cum.T
    step_ref[...], reach_ref[...], bare_ref[...], cum_ref[...] = step, reach, bare, cum
    cumt_ref[...] = cum_rows[:16, :]
    end_ref[...] = jnp.broadcast_to(through, (8, 128))
    rows = lax.broadcasted_iota(jnp.int32, (CHUNK, CHUNK), 0)
    cols = lax.broadcasted_iota(jnp.int32, (CHUNK, CHUNK), 1)
    allowed = (marks[:, 0:1] == row_ref[0:1, :]) & (rows >= cols)
    inner = mm_nt(c, b)
    lanes = lax.broadcasted_iota(jnp.int32, (CHUNK, PAIR), 1)
    subs = lax.broadcasted_iota(jnp.int32, (PAIR, N), 0)
    for p in range(PAIRS):
        span = slice(PAIR * p, PAIR * (p + 1))
        h = 2 * p

        def pick(value):
            return halves(value[:, h : h + 1], value[:, h + 1 : h + 2], lanes)

        conv = taps_ref[0:1, span] * buf[EDGE : EDGE + CHUNK, span]
        for lag in range(1, TAPS):
            moved = buf[EDGE - lag : EDGE - lag + CHUNK, span]
            conv = conv + taps_ref[lag : lag + 1, span] * moved * marks[:, 2 + lag : 3 + lag]
        conv_ref[:, span] = conv
        x = conv * jax.nn.sigmoid(conv)
        scaled = (x * pick(step)).astype(BF16)
        local = []
        for q in (h, h + 1):
            spread = cum[:, q : q + 1] - cum_rows[q : q + 1, :]
            mixing = jnp.exp(jnp.where(allowed, spread, -1e30)) * inner
            local.append(mm(mixing.astype(BF16), scaled))
        held = state[span, :]
        hb = held.astype(BF16)
        st_ref[0, span, :] = hb
        y_ref[:, span] = (
            halves(local[0], local[1], lanes) + pick(reach) * mm_nt(c, hb) + skip_ref[:, span] * x
        )
        tail = mm_tn((pick(weight) * x).astype(BF16), b)
        kept = jnp.where(subs < P_SIZE, through[:, h : h + 1], through[:, h + 1 : h + 2])
        state[span, :] = kept * held + tail


def ssd_backward_kernel(first, *refs):
    (g_ref, x_ref, xp_ref, conv_ref, act_ref, step_ref, reach_ref, bare_ref), refs = refs[:8], refs[8:]
    (cum_ref, cumt_ref, end_ref, st_ref, raw_ref, bias_ref, log_ref), refs = refs[:7], refs[7:]
    (taps_ref, _, mark_ref, row_ref, skip_ref), refs = refs[:5], refs[5:]
    if first:
        (dbc_in, draw_in, _), refs = refs[:3], refs[3:]
    dx_ref, dbc_ref, draw_ref, sums_ref, tsums_ref, later, buf, ahead_buf = refs

    @pl.when(pl.program_id(0) == 0)
    def _():
        later[...] = jnp.zeros_like(later)
        sums_ref[...] = jnp.zeros_like(sums_ref)
        tsums_ref[...] = jnp.zeros_like(tsums_ref)
        ahead_buf[...] = jnp.zeros_like(ahead_buf)

    marks = mark_ref[...]
    buf[0:EDGE, :] = xp_ref[CHUNK - 2 * EDGE :, :].astype(F32)[EDGE:, :]
    buf[EDGE : EDGE + CHUNK, :] = x_ref[...].astype(F32)
    b, c = act_ref[:, :N], act_ref[:, N:]
    step, reach, bare, cum = step_ref[...], reach_ref[...], bare_ref[...], cum_ref[...]
    cum_rows, through = cumt_ref[...], end_ref[0:1, :]
    weight = bare * step
    rows = lax.broadcasted_iota(jnp.int32, (CHUNK, CHUNK), 0)
    cols = lax.broadcasted_iota(jnp.int32, (CHUNK, CHUNK), 1)
    allowed = (marks[:, 0:1] == row_ref[0:1, :]) & (rows >= cols)
    inner = mm_nt(c, b)
    lanes = lax.broadcasted_iota(jnp.int32, (CHUNK, PAIR), 1)
    subs = lax.broadcasted_iota(jnp.int32, (PAIR, N), 0)
    wide = lax.broadcasted_iota(jnp.int32, (CHUNK, 128), 1)
    last = lax.broadcasted_iota(jnp.int32, (CHUNK, 1), 0) == CHUNK - 1
    d_inner = jnp.zeros((CHUNK, CHUNK), F32)
    db = jnp.zeros((CHUNK, N), F32)
    dc = jnp.zeros((CHUNK, N), F32)
    d_cum = jnp.zeros((CHUNK, 128), F32)
    d_step = jnp.zeros((CHUNK, 128), F32)
    ahead_buf[CHUNK : CHUNK + EDGE, :] = ahead_buf[0:EDGE, :]
    count = range(PAIRS // 2)
    spans = [slice(PAIR * p, PAIR * (p + 1)) for p in count]

    def picked(value):
        return [
            halves(value[:, h : h + 1], value[:, h + 1 : h + 2], lanes)
            for h in (2 * (p + first) for p in count)
        ]

    conv = [conv_ref[:, span] for span in spans]
    g = [g_ref[:, span] for span in spans]
    start = [st_ref[0, span, :] for span in spans]
    ahead = [later[span, :].astype(BF16) for span in spans]
    bs = [mm_nt(b, a) for a in ahead]
    cs = [mm_nt(c, a) for a in start]
    sg = [jax.nn.sigmoid(v) for v in conv]
    x = [v * w for v, w in zip(conv, sg)]
    step2, reach2, weight2, bare2 = picked(step), picked(reach), picked(weight), picked(bare)
    scaled = [(v * w).astype(BF16) for v, w in zip(x, step2)]
    e = []
    for q in range(PAIRS):
        spread = cum[:, 2 * first + q : 2 * first + q + 1] - cum_rows[2 * first + q : 2 * first + q + 1, :]
        e.append(jnp.exp(jnp.where(allowed, spread, -1e30)))
    d_mix = []
    for p in count:
        for q in (0, 1):
            mine = (lanes >= P_SIZE) if q else (lanes < P_SIZE)
            d_mix.append(mm_nt(jnp.where(mine, g[p], 0.0).astype(BF16), scaled[p]))
    mixing = [v * inner for v in e]
    local = [mm_tn(mixing[q].astype(BF16), g[q // 2].astype(BF16)) for q in range(PAIRS)]
    totals = []
    for q in range(PAIRS):
        d_inner = d_inner + d_mix[q] * e[q]
        totals.append(jnp.sum(d_mix[q] * mixing[q], axis=1, keepdims=True))
    local = [halves(local[2 * p], local[2 * p + 1], lanes) for p in count]
    gr = [(v * w).astype(BF16) for v, w in zip(reach2, g)]
    wx = [(v * w).astype(BF16) for v, w in zip(weight2, x)]
    for p in count:
        dc = dc + mm(gr[p], start[p])
        db = db + mm(wx[p], ahead[p])
    for p in count:
        h = 2 * (p + first)
        held = later[spans[p], :]
        product = held * start[p].astype(F32)
        kept = jnp.where(subs < P_SIZE, through[:, h : h + 1], through[:, h + 1 : h + 2])
        later[spans[p], :] = kept * held + mm_tn(gr[p], c)
        xbs = x[p] * bs[p]
        xl = x[p] * local[p]
        stored = xbs * weight2[p]
        direct = xbs * bare2[p] + xl
        change = g[p] * cs[p] * reach2[p] - stored - xl * step2[p]
        for q in (0, 1):
            mine = (lanes >= P_SIZE) if q else (lanes < P_SIZE)
            half = slice(P_SIZE * q, P_SIZE * (q + 1))
            stored_sum = jnp.sum(jnp.sum(stored, axis=0, keepdims=True)[:, half], keepdims=True)
            held_sum = jnp.sum(jnp.sum(product[half], axis=0, keepdims=True), keepdims=True)
            end = stored_sum + through[:, h + q : h + q + 1] * held_sum
            cum_q = totals[2 * p + q] + jnp.sum(jnp.where(mine, change, 0.0), axis=1, keepdims=True)
            cum_q = cum_q + jnp.where(last, end, 0.0)
            step_q = jnp.sum(jnp.where(mine, direct, 0.0), axis=1, keepdims=True)
            d_cum = jnp.where(wide == h + q, cum_q, d_cum)
            d_step = jnp.where(wide == h + q, step_q, d_step)
    d_conv = []
    for p in count:
        span = spans[p]
        dx = local[p] * step2[p] + weight2[p] * bs[p] + skip_ref[:, span] * g[p]
        d_conv.append(dx * sg[p] * (1.0 + conv[p] * (1.0 - sg[p])))
        ahead_buf[0:CHUNK, span] = d_conv[p]
    for p in count:
        span = spans[p]
        d_in = taps_ref[0:1, span] * d_conv[p]
        for lag in range(1, TAPS):
            d_in = d_in + taps_ref[lag : lag + 1, span] * (
                ahead_buf[lag : lag + CHUNK, span] * marks[:, 5 + lag : 6 + lag]
            )
        dx_ref[:, span] = d_in.astype(BF16)
        for lag in range(TAPS):
            moved = buf[EDGE - lag : EDGE - lag + CHUNK, span]
            if lag:
                moved = moved * marks[:, 2 + lag : 3 + lag]
            tsums_ref[lag : lag + 1, span] += jnp.sum(d_conv[p] * moved, axis=0, keepdims=True)
        tsums_ref[TAPS : TAPS + 1, span] += jnp.sum(g[p] * x[p], axis=0, keepdims=True)
    di = d_inner.astype(BF16)
    db = db + mm_tn(di, c)
    dc = dc + mm(di, b)
    for q, part in enumerate((db[:, :WB], db[:, WB:], dc[:, :WB], dc[:, WB:])):
        dbc_ref[q] = part + dbc_in[q] if first else part
    upper = (cols >= rows).astype(F32)
    d_decay = jnp.dot(upper, d_cum, precision=HIGHEST, preferred_element_type=F32)
    rate = jnp.exp(log_ref[...])
    d_raw = (d_step - rate * d_decay) * jax.nn.sigmoid(raw_ref[...] + bias_ref[...])
    sums_ref[0:1, :] += jnp.sum(d_raw, axis=0, keepdims=True)
    sums_ref[1:2, :] -= jnp.sum(d_decay * (rate * step), axis=0, keepdims=True)
    draw_ref[...] = d_raw + draw_in[...] if first else d_raw


def ssd_specs(chunks, flip, width, part):
    def at(i):
        return chunks - 1 - i if flip else i

    def rowwise(size, col=0):
        return pl.BlockSpec((CHUNK, size), lambda i: (at(i), col))

    def fixed(height, size, col=0):
        return pl.BlockSpec((height, size), lambda i: (0, col))

    def behind(size, col=0):
        return pl.BlockSpec((CHUNK, size), lambda i: (jnp.maximum(at(i) - 1, 0), col))

    def across(height):
        return pl.BlockSpec((height, CHUNK), lambda i: (0, at(i)))

    states = pl.BlockSpec((1, width, N), lambda i: (at(i), part, 0))
    dbc = pl.BlockSpec((NC, CHUNK, WB), lambda i: (0, at(i), 0))
    end = pl.BlockSpec((8, 128), lambda i: (at(i), 0))
    kept = [rowwise(width, part), rowwise(2 * N)] + [rowwise(128)] * 4 + [across(16), end]
    tail = [
        rowwise(128), fixed(1, 128), fixed(1, 128), fixed(TAPS, width, part), fixed(TAPS, 2 * N),
        rowwise(16), across(8), fixed(1, width, part),
    ]
    return rowwise, fixed, behind, states, dbc, kept, tail


def ssd_forward(x, bc, *rest):
    tokens = x.shape[0]
    chunks = tokens // CHUNK
    rowwise, _, _, states, _, kept, tail = ssd_specs(chunks, False, WX, 0)
    by_token = jax.ShapeDtypeStruct((tokens, 128), F32)
    y, states, *saved = pl.pallas_call(
        ssd_forward_kernel,
        grid=(chunks,),
        in_specs=[rowwise(WX), rowwise(2 * N)] + tail,
        out_specs=[rowwise(WX), states] + kept,
        out_shape=[
            jax.ShapeDtypeStruct((tokens, WX), F32),
            jax.ShapeDtypeStruct((chunks, WX, N), BF16),
            jax.ShapeDtypeStruct((tokens, WX), F32),
            jax.ShapeDtypeStruct((tokens, 2 * N), BF16),
            by_token,
            by_token,
            by_token,
            by_token,
            jax.ShapeDtypeStruct((16, tokens), F32),
            jax.ShapeDtypeStruct((8 * chunks, 128), F32),
        ],
        scratch_shapes=[
            pltpu.VMEM((WX, N), F32),
            pltpu.VMEM((CHUNK + EDGE, WX), F32),
            pltpu.VMEM((CHUNK + EDGE, 2 * N), F32),
        ],
        compiler_params=pltpu.CompilerParams(
            dimension_semantics=("arbitrary",), vmem_limit_bytes=40 << 20
        ),
        name="ssd_forward",
    )(x, bc, *rest)
    return y, (*saved, states)


def ssd_backward(part, g, x, saved, rest, earlier=()):
    tokens = x.shape[0]
    chunks = tokens // CHUNK
    half = WX // 2
    rowwise, fixed, behind, st, dbc, kept, tail = ssd_specs(chunks, True, half, part)
    extra = [dbc, rowwise(128), pl.BlockSpec(memory_space=pl.ANY)] if part else []
    return pl.pallas_call(
        functools.partial(ssd_backward_kernel, part * PAIRS // 2),
        grid=(chunks,),
        in_specs=[rowwise(half, part), rowwise(half, part), behind(half, part)]
        + kept
        + [st]
        + tail
        + extra,
        out_specs=[rowwise(half, part), dbc, rowwise(128), fixed(8, 128), fixed(8, half)],
        out_shape=[
            jax.ShapeDtypeStruct((tokens, WX), BF16),
            jax.ShapeDtypeStruct((NC, tokens, WB), F32),
            jax.ShapeDtypeStruct((tokens, 128), F32),
            jax.ShapeDtypeStruct((8, 128), F32),
            jax.ShapeDtypeStruct((8, half), F32),
        ],
        scratch_shapes=[
            pltpu.VMEM((half, N), F32),
            pltpu.VMEM((CHUNK + EDGE, half), F32),
            pltpu.VMEM((CHUNK + EDGE, half), F32),
        ],
        input_output_aliases={22: 0} if part else {},
        compiler_params=pltpu.CompilerParams(
            dimension_semantics=("arbitrary",), vmem_limit_bytes=40 << 20
        ),
        name="ssd_backward",
    )(g, x, x, *saved, *rest, *earlier)


Q_BLOCK = 256
SCALE = HEAD_SIZE ** (-0.5)


def attention_probs(q, k, segc, segr, i):
    scores = mm_nt(q, k) * SCALE
    rows = lax.broadcasted_iota(jnp.int32, scores.shape, 0) + i * Q_BLOCK
    cols = lax.broadcasted_iota(jnp.int32, scores.shape, 1)
    scores = jnp.where((rows >= cols) & (segc == segr), scores, -1e30)
    grown = jnp.exp(scores - jnp.max(scores, axis=-1, keepdims=True))
    return grown / jnp.sum(grown, axis=-1, keepdims=True)


def attention_forward_kernel(q_ref, k_ref, v_ref, segc_ref, segr_ref, o_ref):
    probs = attention_probs(q_ref[...], k_ref[...], segc_ref[...], segr_ref[...], pl.program_id(1))
    o_ref[...] = mm(probs.astype(BF16), v_ref[...]).astype(BF16)


def attention_backward_kernel(
    q_ref, k_ref, v_ref, segc_ref, segr_ref, g_ref, dq_ref, dk_ref, dv_ref
):
    @pl.when((pl.program_id(0) == 0) & (pl.program_id(1) == 0))
    def _():
        dk_ref[...] = jnp.zeros_like(dk_ref)
        dv_ref[...] = jnp.zeros_like(dv_ref)

    q, k, g = q_ref[...], k_ref[...], g_ref[...]
    probs = attention_probs(q, k, segc_ref[...], segr_ref[...], pl.program_id(1))
    d_probs = mm_nt(g, v_ref[...])
    inner = jnp.sum(probs * d_probs, axis=-1, keepdims=True)
    d_scores = (probs * (d_probs - inner)).astype(BF16)
    dq_ref[...] = mm(d_scores, k) * SCALE
    dk_ref[...] += mm_tn(d_scores, q) * SCALE
    dv_ref[...] += mm_tn(probs.astype(BF16), g)


def attention_specs(tokens):
    block = pl.BlockSpec((Q_BLOCK, HEAD_SIZE), lambda h, i: (i, h))
    whole = pl.BlockSpec((tokens, HEAD_SIZE), lambda h, i: (0, 0))
    segc = pl.BlockSpec((Q_BLOCK, 1), lambda h, i: (i, 0))
    segr = pl.BlockSpec((1, tokens), lambda h, i: (0, 0))
    params = pltpu.CompilerParams(
        dimension_semantics=("arbitrary", "arbitrary"), vmem_limit_bytes=32 << 20
    )
    return block, whole, segc, segr, params


def attention_forward(q, k, v, segc, segr):
    tokens = q.shape[0]
    block, whole, sc, sr, params = attention_specs(tokens)
    return pl.pallas_call(
        attention_forward_kernel,
        grid=(QH, tokens // Q_BLOCK),
        in_specs=[block, whole, whole, sc, sr],
        out_specs=block,
        out_shape=jax.ShapeDtypeStruct((tokens, QH * HEAD_SIZE), BF16),
        compiler_params=params,
        name="attention_forward",
    )(q, k, v, segc, segr)


def attention_backward(q, k, v, segc, segr, g):
    tokens = q.shape[0]
    block, whole, sc, sr, params = attention_specs(tokens)
    return pl.pallas_call(
        attention_backward_kernel,
        grid=(QH, tokens // Q_BLOCK),
        in_specs=[block, whole, whole, sc, sr, block],
        out_specs=[block, whole, whole],
        out_shape=[
            jax.ShapeDtypeStruct((tokens, QH * HEAD_SIZE), F32),
            jax.ShapeDtypeStruct((tokens, HEAD_SIZE), F32),
            jax.ShapeDtypeStruct((tokens, HEAD_SIZE), F32),
        ],
        compiler_params=params,
        name="attention_backward",
    )(q, k, v, segc, segr, g)


def rms_of(rows):
    return lax.rsqrt(jnp.mean(rows * rows, axis=-1, keepdims=True) + NORM_EPSILON)


def norm_back(grad, rows, r, gain):
    w = grad * gain
    return r * w - rows * (r * r * r) * jnp.mean(w * rows, axis=-1, keepdims=True)


def silu_slope(value):
    sg = jax.nn.sigmoid(value)
    return sg * (1.0 + value * (1.0 - sg))


def turned(heads, cosine, sine):
    half = HEAD_SIZE // 2
    parts = []
    for h in range(heads.shape[1] // HEAD_SIZE):
        v = heads[:, h * HEAD_SIZE : (h + 1) * HEAD_SIZE]
        parts.append(v * cosine + jnp.concatenate([v[:, half:], v[:, :half]], axis=1) * sine)
    return jnp.concatenate(parts, axis=1)


def shifted(value, lag):
    if lag == 0:
        return value
    zeros = jnp.zeros((abs(lag), value.shape[1]), value.dtype)
    if lag > 0:
        return jnp.concatenate([zeros, value[:-lag]], axis=0)
    return jnp.concatenate([value[-lag:], zeros], axis=0)


def convolve(value, taps, keeps):
    total = taps[0][None] * value
    for lag in range(1, TAPS):
        total = total + taps[lag][None] * shifted(value, lag) * keeps[lag]
    return total


def body(
    tokens,
    segment_ids,
    valid_mask,
    teacher,
    mixer_in,
    mixer_out,
    query_weight,
    key_value_weight,
    output_weight,
    gate_up,
    down_weight,
    norm_first,
    norm_second,
    conv_taps,
    decay_log,
    skip_gain,
    step_bias,
):
    ring = Ring()
    nb = ring.n
    j = lax.axis_index("ctx")
    own = tokens.shape[0] * tokens.shape[1]
    length = own * NC
    devices = nb * NC
    total_tokens = float(own * devices)
    x = tokens.reshape(own, MODEL_WIDTH).astype(F32)
    valid = valid_mask.reshape(own).astype(F32)
    target = teacher.reshape(own, MODEL_WIDTH).astype(F32)

    order = Order(jnp.broadcast_to(valid[:1] * 0.0, (8, 128)))
    gate, scale = order.gate, max(1, nb // 8)

    def turn(run, *others):
        for _ in range(scale):
            if not run.over:
                others = run.turn(others)
        return others[0] if len(others) == 1 else others

    def finish(run, *others):
        while not run.over:
            others = run.turn(others)
        return others[0] if len(others) == 1 else others

    def start(block, place=lambda b: b):
        return GatherRun(ring, order, block, place)

    rows = mixer_in.shape[0]
    edge = 2 * DI + 2 * N
    unit = down_weight.shape[0]
    near_seg = Near(segment_ids.reshape(1, own))
    g_down = start(down_weight)
    rows_out, rows_attn = mixer_out.shape[0], output_weight.shape[0]

    def home(q):
        return (q % 2) * 4 + q // 2 % 2 * 2 + q // 4 if nb == 8 else q

    there = [(m, home(m % nb) * NC + m // nb) for m in range(devices)]
    back = [(b, a) for a, b in there]
    both_out = lax.ppermute(
        jnp.concatenate([mixer_out, output_weight], axis=0), ("batch", "ctx"), there
    )
    xs_cols = mixer_in[:, DI : 2 * DI].reshape(rows, NC, WX)
    bc_cols = mixer_in[:, 2 * DI : edge].reshape(rows, NC, WB)
    dt_cols = mixer_in[:, edge:].reshape(rows, NC, HEADS)
    digits = jnp.sum(valid)
    digits = jnp.stack([jnp.floor(digits / 64.0), digits % 64.0]).astype(BF16)
    shape = (rows, NC, 128 - HEADS)
    lane = lax.broadcasted_iota(jnp.int32, shape, 2) - (126 - HEADS)
    lane = jnp.where(lax.broadcasted_iota(jnp.int32, shape, 0) == 0, lane, -1)
    padding = jnp.where(lane == 0, digits[0], jnp.where(lane == 1, digits[1], 0))
    dt_cols = jnp.concatenate([dt_cols, padding.astype(BF16)], axis=2)
    first_cols = jnp.concatenate([xs_cols, bc_cols, dt_cols], axis=2).transpose(1, 0, 2)
    spread = Spread(first_cols, j)
    spread.got, mixer_in, query_weight, key_value_weight, x, near_seg.far, near_seg.next = turn(
        g_down, spread.got, mixer_in, query_weight, key_value_weight, x, near_seg.far,
        near_seg.next
    )
    spread.cross()
    near_seg.cross()
    z_cols = mixer_in[:, :DI].reshape(rows, NC, WX)
    q_cols = query_weight.reshape(rows, NC, WQ)
    kv = key_value_weight.reshape(rows, 2, 2, HEAD_SIZE)
    kv_cols = kv.transpose(0, 2, 1, 3).reshape(rows, NC, HEAD_SIZE)
    second_cols = jnp.concatenate([q_cols, kv_cols, z_cols], axis=2).transpose(1, 0, 2)
    spread_two = Spread(second_cols, j)
    (spread.across, x) = gate(spread.across, x)
    g_first = start(spread.block())
    r_x = rms_of(x)
    normed_own = (x * r_x * norm_first).astype(BF16)
    near_normed = Near(normed_own)
    spread_two.got, near_normed.next = turn(g_down, spread_two.got, near_normed.next)
    spread_two.cross()
    gate_up, both_out = turn(g_first, gate_up, both_out)
    spread_two.across = turn(g_down, spread_two.across)
    gu_cols = (
        gate_up.reshape(rows, 2, nb, NC, unit).transpose(3, 0, 1, 2, 4).reshape(NC, rows, 2 * WF)
    )
    spread_gu = Spread(gu_cols, j)
    near_normed.far, near_seg.last = turn(g_first, near_normed.far, near_seg.last)
    near_normed.cross()
    g_second = start(spread_two.block())
    (near_normed.last,) = gate(near_normed.last)
    normed = absolute(near_normed.blocks(), j).reshape(length, MODEL_WIDTH)
    place = jnp.arange(length, dtype=jnp.int32)
    normed, conv_taps, decay_log, skip_gain, step_bias, place = finish(
        g_down, normed, conv_taps, decay_log, skip_gain, step_bias, place
    )
    w_down = g_down.whole

    seg = absolute(near_seg.blocks(), j).reshape(length)
    keeps, marks_ahead = [None], []
    for lag in range(1, TAPS):
        before = jnp.concatenate([jnp.full((lag,), -1, jnp.int32), seg[:-lag]])
        after_it = jnp.concatenate([seg[lag:], jnp.full((lag,), -1, jnp.int32)])
        keeps.append((before == seg).astype(F32))
        marks_ahead.append((after_it == seg).astype(F32))
    chunks = length // CHUNK
    seg_f = seg.astype(F32)
    seg_last = seg_f.reshape(chunks, CHUNK)[:, -1]
    seg_prev = jnp.concatenate([jnp.full((1,), -1.0, F32), seg_last[:-1]])
    marks = jnp.stack(
        [seg_f, jnp.repeat(seg_prev, CHUNK), jnp.repeat(seg_last, CHUNK)] + keeps[1:] + marks_ahead
        + [jnp.zeros_like(seg_f)] * 7
    ).T
    row = jnp.broadcast_to(seg_f[None, :], (8, length))
    keeps = [None] + [marks[:, 2 + lag : 3 + lag] for lag in range(1, TAPS)]
    marks, row, spread_gu.got = turn(g_first, marks, row, spread_gu.got)
    spread_gu.cross()
    half = HEAD_SIZE // 2
    inverse = ROPE_BASE ** (-(jnp.arange(half, dtype=F32) * 2.0) / HEAD_SIZE)
    angle = place.astype(F32)[:, None] * inverse[None, :]
    cosine, sine = jnp.cos(angle), jnp.sin(angle)
    cosine = jnp.concatenate([cosine, cosine], axis=1)
    sine = jnp.concatenate([-sine, sine], axis=1)
    heads_at = j * HEADS
    lane_pad = ((0, 0), (0, 128 - HEADS))
    own_log = jnp.pad(lax.dynamic_slice_in_dim(decay_log, heads_at, HEADS)[None], lane_pad)
    own_bias = jnp.pad(lax.dynamic_slice_in_dim(step_bias, heads_at, HEADS)[None], lane_pad)
    own_skip = lax.dynamic_slice_in_dim(skip_gain, heads_at, HEADS)
    skip_wide = jnp.repeat(own_skip, P_SIZE)[None, :]
    taps_x = lax.dynamic_slice(conv_taps, (0, j * WX), (TAPS, WX))
    taps_b = conv_taps[:, DI:]
    taps_b_own = lax.dynamic_slice(conv_taps, (0, DI + j * WB), (TAPS, WB))
    cosine, sine, normed = finish(g_first, cosine, sine, normed)
    w_first = g_first.whole
    digits = jnp.sum(w_first[::rows, -2:].astype(F32), axis=0)
    count = digits[0] * 64.0 + digits[1]
    lane = jnp.arange(128)[None, :]
    w_raw = jnp.where(lane < HEADS, w_first[:, WX + WB :], 0)

    conv_b_own = mm(normed, w_first[:, WX : WX + WB]).astype(BF16)
    b_far = y_swap(conv_b_own)
    conv_b_own, normed, w_first = turn(g_second, conv_b_own, normed, w_first)
    step_raw = mm(normed, w_raw)
    conv_x = mm(normed, w_first[:, :WX]).astype(BF16)
    conv_x, step_raw, b_far = turn(g_second, conv_x, step_raw, b_far)
    b_other = core_swap(jnp.concatenate([conv_b_own, b_far], axis=1))
    g_out = start(both_out, lambda b: home(b))
    upper, core = j // 2, j % 2
    mine = (jnp.where(upper == 0, conv_b_own, b_far), jnp.where(upper == 0, b_far, conv_b_own))
    b_other = turn(g_second, b_other)
    theirs = (
        jnp.where(upper == 0, b_other[:, :WB], b_other[:, WB:]),
        jnp.where(upper == 0, b_other[:, WB:], b_other[:, :WB]),
    )
    conv_b = jnp.concatenate(
        [
            jnp.where(core == 0, mine[0], theirs[0]),
            jnp.where(core == 0, theirs[0], mine[0]),
            jnp.where(core == 0, mine[1], theirs[1]),
            jnp.where(core == 0, theirs[1], mine[1]),
        ],
        axis=1,
    )
    rest_ssd = (step_raw, own_bias, own_log, taps_x, taps_b, marks, row, skip_wide)
    ssm_y, saved = ssd_forward(conv_x, conv_b, *rest_ssd)
    ssm_y, normed, spread_gu.across = finish(g_second, ssm_y, normed, spread_gu.across)
    w_second = g_second.whole
    normed = turn(g_out, normed)
    rest = mm(normed, w_second)
    gate_z = rest[:, WQ + HEAD_SIZE :]
    queries = turned(rest[:, :WQ], cosine, sine).astype(BF16)
    kv_raw = rest[:, WQ : WQ + HEAD_SIZE]
    kv_own = jnp.where(core == 0, turned(kv_raw, cosine, sine), kv_raw).astype(BF16)
    kv_other = core_swap(kv_own)
    queries, kv_own, kv_other, gate_z = turn(g_out, queries, kv_own, kv_other, gate_z)
    g_gu = start(spread_gu.block())
    keys = jnp.where(core == 0, kv_own, kv_other)
    values = jnp.where(core == 0, kv_other, kv_own)
    segc, segr = seg[:, None], seg[None, :]
    attended = attention_forward(queries, keys, values, segc, segr)
    silu_z = jax.nn.silu(gate_z)
    gated = (ssm_y * silu_z).astype(BF16)
    attended, gated = turn(g_out, attended, gated)
    acts = jnp.concatenate([gated, attended], axis=1)
    acts = finish(g_out, acts)
    out_all = g_out.whole.reshape(nb, rows_out + rows_attn, MODEL_WIDTH)
    w_out = jnp.concatenate(
        [
            out_all[:, :rows_out].reshape(WX, MODEL_WIDTH),
            out_all[:, rows_out:].reshape(WQ, MODEL_WIDTH),
        ],
        axis=0,
    )


    def upper_rows(value, far):
        return lax.dynamic_slice_in_dim(value, (1 - upper if far else upper) * 2 * own, 2 * own)

    def in_two(value):
        return value.reshape(2, own, -1)

    mixed = NearSum(lambda far: in_two(mm(upper_rows(acts, far), w_out)), core)
    mixed.first, mixed.near = turn(g_gu, mixed.first, mixed.near)
    (mixed.second,) = gate(mixed.second)
    hidden_one = x + mixed.result()
    r_h = rms_of(hidden_one)
    normed_two_own = (hidden_one * r_h * norm_second).astype(BF16)
    (normed_two_own,) = gate(normed_two_own)
    near_two = Near(normed_two_own)
    near_two.next = turn(g_gu, near_two.next)
    near_two.far = turn(g_gu, near_two.far)
    near_two.cross()
    normed_two = near_two.blocks()
    normed_two_all = stacked(normed_two)
    normed_two = list(finish(g_gu, *normed_two))
    w_gu = g_gu.whole

    gates = {}
    hidden_all = jnp.zeros((length, WF), BF16)
    for k in reversed(range(NC)):
        gateup = mm(normed_two[k], w_gu)
        gates[k] = gateup
        piece = (jax.nn.silu(gateup[:, :WF]) * gateup[:, WF:]).astype(BF16)
        hidden_all = lax.dynamic_update_slice(hidden_all, piece, (k * own, 0))

    def near_rows(value, far):
        return value[2 * own :] if far else value[: 2 * own]

    ffn = NearSum(lambda far: in_two(mm(near_rows(hidden_all, far), w_down)), 0)
    (ffn.second,) = gate(ffn.second)
    final = hidden_one + ffn.result()
    error = final - target
    squares = jnp.sum(valid * jnp.sum(error * error, axis=1))
    grad_final = valid[:, None] * error * (total_tokens / count)
    grad_ffn_own = grad_final.astype(BF16)

    def reduce(left, right):
        whole = mm_tn(left, right).astype(BF16)
        size = whole.shape[0] // nb

        def part(slot):
            return lax.dynamic_slice_in_dim(whole, ring.owner(slot) * size, size)

        return ReduceRun(ring, order, part)

    (grad_ffn_own,) = gate(grad_ffn_own)
    near_ffn = Near(grad_ffn_own)
    d_gateup_all = jnp.zeros((length, 2 * WF), BF16)

    def ffn_back(whole, grad, k):
        d_hidden = mm_nt(grad, w_down)
        gate_k, up_k = gates[k][:, :WF], gates[k][:, WF:]
        d_gate = (d_hidden * up_k * silu_slope(gate_k)).astype(BF16)
        d_up = (d_hidden * jax.nn.silu(gate_k)).astype(BF16)
        whole = lax.dynamic_update_slice(whole, d_gate, (k * own, 0))
        return lax.dynamic_update_slice(whole, d_up, (k * own, WF))

    d_gateup_all = ffn_back(d_gateup_all, near_ffn.own, 0)
    d_gateup_all = ffn_back(d_gateup_all, near_ffn.next, 1)
    near_ffn.far, near_ffn.next, near_ffn.own, d_gateup_all = gate(
        near_ffn.far, near_ffn.next, near_ffn.own, d_gateup_all
    )
    near_ffn.cross()
    d_gateup_all = ffn_back(d_gateup_all, near_ffn.far, 2)
    d_gateup_all, near_ffn.last = gate(d_gateup_all, near_ffn.last)
    grad_ffn_all = stacked(near_ffn.blocks())
    r_down = reduce(hidden_all, grad_ffn_all)
    d_gateup_all = ffn_back(d_gateup_all, near_ffn.last, 3)
    (d_gateup_all,) = gate(d_gateup_all)

    d_gateup_all = turn(r_down, d_gateup_all)
    held = [d_gateup_all]
    two = NearSum(lambda far: in_two(mm_nt(near_rows(held[0], far), w_gu)), 0, True)
    two.third, d_gateup_all = gate(two.third, d_gateup_all)
    held = [d_gateup_all]
    two.go()
    two.stay()
    two.first, two.near = turn(r_down, two.first, two.near)
    two.near, two.second = gate(two.near, two.second)
    grad_normed_two = two.result()
    w_two = norm_back(grad_normed_two, hidden_one, r_h, norm_second)
    g_norm_second = jnp.sum(grad_normed_two * hidden_one * r_h, axis=0)
    grad_hidden_one = grad_final + w_two
    branch_own = grad_hidden_one.astype(BF16)
    branch_own, grad_hidden_one, g_norm_second = gate(branch_own, grad_hidden_one, g_norm_second)
    near_branch = Near(branch_own)
    near_branch.next, d_gateup_all = turn(r_down, near_branch.next, d_gateup_all)
    r_gu = reduce(normed_two_all, d_gateup_all)
    near_branch.far = finish(r_down, near_branch.far)
    near_branch.cross()
    (near_branch.last,) = gate(near_branch.last)
    branch = absolute(near_branch.blocks(), j).reshape(length, MODEL_WIDTH)
    d_acts = mm_nt(branch, w_out)
    grad_attended = d_acts[:, WX:].astype(BF16)
    grad_gated = d_acts[:, :WX]
    grad_ssm_y = grad_gated * silu_z
    d_z = (grad_gated * ssm_y * silu_slope(gate_z)).astype(BF16)
    grad_attended, grad_ssm_y, d_z, branch = gate(grad_attended, grad_ssm_y, d_z, branch)

    out_whole = mm_tn(acts, branch).astype(BF16)

    def out_part(slot):
        b = home(ring.owner(slot))
        return jnp.concatenate(
            [
                lax.dynamic_slice_in_dim(out_whole, b * rows_out, rows_out),
                lax.dynamic_slice_in_dim(out_whole, WX + b * rows_attn, rows_attn),
            ],
            axis=0,
        )

    r_out = ReduceRun(ring, order, out_part)
    grad_attended = turn(r_gu, grad_attended)

    dq, dk, dv = attention_backward(queries, keys, values, segc, segr, grad_attended)
    sent = jnp.where(core == 0, dv, dk)
    d_kv_other = core_swap(sent)
    dq, dk, dv, d_kv_other = turn(r_out, dq, dk, dv, d_kv_other)
    d_query = turned(dq, cosine, -sine).astype(BF16)
    d_kv = jnp.where(core == 0, dk, dv) + d_kv_other
    d_kv = jnp.where(core == 0, turned(d_kv, cosine, -sine), d_kv).astype(BF16)
    d_second = jnp.concatenate([d_query, d_kv, d_z], axis=1)
    r_second = reduce(normed, d_second)

    def collected(run):
        return Collect(run.result.astype(BF16).reshape(NC, rows, run.result.shape[1]), j)

    grad_ssm_y, d_second = turn(r_gu, grad_ssm_y, d_second)
    d_early = mm_nt(d_second, w_second)
    operands = (grad_ssm_y, conv_x, saved, rest_ssd)
    d_in_x, dbc, d_raw, sums_a, tsums_a = ssd_backward(0, *operands)
    d_in_x, dbc, d_raw = turn(r_out, d_in_x, dbc, d_raw)
    d_in_x, dbc, d_raw = turn(r_second, d_in_x, dbc, d_raw)
    d_in_x, dbc, d_raw = turn(r_gu, d_in_x, dbc, d_raw)
    d_in_x, dbc, d_raw, sums_b, tsums_b = ssd_backward(1, *operands, (dbc, d_raw, d_in_x))
    d_in_x, dbc, d_raw = turn(r_second, d_in_x, dbc, d_raw)
    d_in_x, dbc, d_raw = turn(r_out, d_in_x, dbc, d_raw)
    d_bc = dbc.reshape(2, 2, length, WB)
    b_sum = NearSum(lambda far: d_bc[1 - upper if far else upper], core)
    b_sum.near = finish(r_gu, b_sum.near)
    col_gu = collected(r_gu)
    sums = sums_a + sums_b
    tsums = jnp.concatenate([tsums_a, tsums_b], axis=1)
    g_bias, g_log = sums[0, :HEADS], sums[1, :HEADS]
    g_taps_x = tsums[:TAPS]
    g_skip = jnp.sum(tsums[TAPS].reshape(HEADS, P_SIZE), axis=1)

    def conv_back(d_conv, value, taps):
        d_in = taps[0][None] * d_conv
        g_taps = [jnp.sum(d_conv * value, axis=0)]
        for lag in range(1, TAPS):
            masked = d_conv * keeps[lag]
            d_in = d_in + taps[lag][None] * shifted(masked, -lag)
            g_taps.append(jnp.sum(masked * shifted(value, lag), axis=0))
        return d_in.astype(BF16), jnp.stack(g_taps)

    b_sum.second, b_sum.near, b_sum.first, conv_b_own, taps_b_own, col_gu.got = turn(
        r_second, b_sum.second, b_sum.near, b_sum.first, conv_b_own, taps_b_own, col_gu.got
    )
    col_gu.cross()
    conv_b_wide = conv_b_own.astype(F32)
    conv_out_b = convolve(conv_b_wide, taps_b_own, keeps)
    d_in_b, g_taps_b = conv_back(b_sum.result() * silu_slope(conv_out_b), conv_b_wide, taps_b_own)
    d_first = jnp.concatenate(
        [d_in_x, d_in_b, d_raw.astype(BF16)], axis=1
    )
    r_first = reduce(normed, d_first)
    d_first = finish(r_out, d_first)
    d_first, col_gu.far = finish(r_second, d_first, col_gu.far)
    col_second = collected(r_second)
    d_first, col_second.got, out_kept = turn(
        r_first, d_first, col_second.got, r_out.result.astype(BF16)
    )
    col_second.cross()
    out_home = lax.ppermute(out_kept, ("batch", "ctx"), back)

    held = [d_first]
    gain_parts = []

    def normed_part(far):
        addends = in_two(mm_nt(upper_rows(held[0], far), w_first) + upper_rows(d_early, far))
        scaled = upper_rows(normed, far).astype(F32).reshape(addends.shape)
        gain_parts.append(jnp.sum(addends * scaled, axis=(0, 1)))
        return addends

    back_sum = NearSum(normed_part, core, True)
    back_sum.third, d_first = gate(back_sum.third, d_first)
    held = [d_first]
    back_sum.go()
    back_sum.stay()
    g_norm_first = (gain_parts[0] + gain_parts[1]) / norm_first
    back_sum.near, g_norm_first, col_second.far, out_home = turn(
        r_first, back_sum.near, g_norm_first, col_second.far, out_home
    )
    taps_all = jnp.zeros((TAPS, DI + 2 * N), F32)
    taps_all = lax.dynamic_update_slice(taps_all, g_taps_x, (0, j * WX))
    taps_all = lax.dynamic_update_slice(taps_all, g_taps_b, (0, DI + j * WB))
    per_head = lax.dynamic_update_slice(
        jnp.zeros((3, 128), F32), jnp.stack([g_log, g_skip, g_bias]), (0, heads_at)
    )
    small = jnp.concatenate(
        [
            g_norm_first.reshape(-1, 128),
            g_norm_second.reshape(-1, 128),
            taps_all.reshape(-1, 128),
            per_head,
            jnp.broadcast_to(squares, (1, 128)),
        ]
    )
    moves = [("batch", nb, 1 << q) for q in range(nb.bit_length() - 1)]
    moves += [("ctx", NC, 1), ("ctx", NC, 2)]
    for axis, size, bit in moves:
        small = small + lax.ppermute(small, axis, [(q, q ^ bit) for q in range(size)])
    back_sum.first = turn(r_first, back_sum.first)
    back_sum.second, back_sum.first = gate(back_sum.second, back_sum.first)
    grad_normed = back_sum.result()
    grad_tokens = grad_hidden_one + norm_back(grad_normed, x, r_x, norm_first)
    grad_tokens = finish(r_first, grad_tokens)
    col_first = collected(r_first)
    col_first.got, small, grad_tokens = gate(col_first.got, small, grad_tokens)
    lines = MODEL_WIDTH // 128
    g_norm_first = small[:lines].reshape(MODEL_WIDTH)
    g_norm_second = small[lines : 2 * lines].reshape(MODEL_WIDTH)
    taps_all = small[2 * lines : -4].reshape(TAPS, DI + 2 * N)
    per_head = small[-4:-1, :H_M]
    loss_value = small[-1, 0] / (MODEL_WIDTH * count) + order.token[0, 0]
    col_first.cross()

    got_gu = col_gu.result()
    grad_gate_up = (
        got_gu.reshape(NC, rows, 2, nb, unit).transpose(1, 2, 3, 0, 4).reshape(rows, 2 * FF)
    )
    got_second = col_second.result()
    got_first = col_first.result()

    def columns(got, begin, size):
        return got[:, :, begin : begin + size].transpose(1, 0, 2).reshape(rows, NC * size)

    grad_query = columns(got_second, 0, WQ)
    grad_keyval = (
        got_second[:, :, WQ : WQ + HEAD_SIZE]
        .reshape(2, 2, rows, HEAD_SIZE)
        .transpose(2, 1, 0, 3)
        .reshape(rows, 4 * HEAD_SIZE)
    )
    grad_mixer_in = jnp.concatenate(
        [
            columns(got_second, WQ + HEAD_SIZE, WX),
            columns(got_first, 0, WX),
            columns(got_first, WX, WB),
            columns(got_first, WX + WB, HEADS),
        ],
        axis=1,
    )
    output = final.astype(BF16).reshape(tokens.shape)
    return (
        output,
        loss_value,
        grad_tokens.reshape(tokens.shape),
        grad_mixer_in,
        out_home[:rows_out].astype(F32),
        grad_query,
        grad_keyval,
        out_home[rows_out:].astype(F32),
        grad_gate_up,
        r_down.result,
        g_norm_first,
        g_norm_second,
        taps_all,
        per_head[0],
        per_head[1],
        per_head[2],
    )


def solution(mesh):
    split_rows = P(("batch", "ctx"), None)
    by_token = P("batch", "ctx", None)
    return jax.shard_map(
        body,
        mesh=mesh,
        in_specs=(by_token, P("batch", "ctx"), P("batch", "ctx"), by_token)
        + (split_rows,) * 7
        + (P(),) * 6,
        out_specs=(by_token, P(), by_token) + (split_rows,) * 7 + (P(),) * 6,
        check_vma=False,
    )
```

```python
import functools

import jax
import jax.numpy as jnp
from jax import lax
from jax.experimental import pallas as pl
from jax.experimental.pallas import tpu as pltpu
from jax.sharding import PartitionSpec as P

MODEL_WIDTH = 2048
H_M = 48
P_SIZE = 64
N = 256
QUERY_HEADS = 8
KEY_VALUE_HEADS = 2
HEAD_SIZE = 128
FF = 4096
TAPS = 4
DI = 3072

NC = 4
HEADS = H_M // NC
PAIRS = HEADS // 2
WX = DI // NC
WB = 2 * N // NC
WQ = QUERY_HEADS * HEAD_SIZE // NC
QH = QUERY_HEADS // NC
WF = FF // NC
CHUNK = 128

NORM_EPSILON = 1e-05
ROPE_BASE = 1000000.0
HIGHEST = lax.Precision.HIGHEST
F32 = jnp.float32
BF16 = jnp.bfloat16


def mm(left, right):
    return jnp.dot(left, right, preferred_element_type=F32)


def mm_tn(left, right):
    return lax.dot_general(left, right, (((0,), (0,)), ((), ())), preferred_element_type=F32)


def mm_nt(left, right):
    return lax.dot_general(left, right, (((1,), (1,)), ((), ())), preferred_element_type=F32)


def after(value, *deps):
    return lax.optimization_barrier((value,) + deps)[0]


def core_swap(value):
    return lax.ppermute(value, "ctx", [(i, i ^ 1) for i in range(NC)])


def y_swap(value):
    return lax.ppermute(value, "ctx", [(i, i ^ 2) for i in range(NC)])


class Ring:
    def __init__(self):
        self.n = lax.axis_size("batch")
        n = self.n
        order = list(range(0, n, 2)) + list(range(n - 1, 0, -2))
        self.up_pairs = [(order[i], order[(i + 1) % n]) for i in range(n)]
        self.down_pairs = [(order[(i + 1) % n], order[i]) for i in range(n)]
        b = lax.axis_index("batch")
        self.pos = jnp.where(b % 2 == 0, b // 2, n - 1 - b // 2)

    def up(self, value):
        return lax.ppermute(value, "batch", self.up_pairs)

    def down(self, value):
        return lax.ppermute(value, "batch", self.down_pairs)

    def owner(self, slot):
        p = (self.pos + slot + self.n) % self.n
        return jnp.where(p < self.n // 2, 2 * p, 2 * (self.n - 1 - p) + 1)


class Order:
    def __init__(self, token):
        self.token = token

    def gate(self, *values):
        out = lax.optimization_barrier(values + (self.token,))
        self.token = out[-1]
        return out[:-1]


class GatherRun:
    def __init__(self, ring, order, block, place=lambda b: b):
        self.ring, self.order, self.place = ring, order, place
        self.rows, cols = block.shape
        (block,) = order.gate(block)
        self.down, self.up = ring.down(block), ring.up(block)
        self.whole = jnp.zeros((ring.n * self.rows, cols), block.dtype)
        self.put(block, 0)
        self.step, self.over = 1, False

    def put(self, part, slot, offset=0):
        at = self.place(self.ring.owner(slot)) * self.rows + offset
        self.whole = lax.dynamic_update_slice(self.whole, part, (at, 0))

    def turn(self, others):
        ring, far, half = self.ring, self.ring.n // 2, self.rows // 2
        down, up, *others = self.order.gate(self.down, self.up, *others)
        if self.step < far:
            if self.step + 1 < far:
                self.down, self.up = ring.down(down), ring.up(up)
            else:
                self.down, self.up = ring.down(down[half:]), ring.up(up[:half])
            self.put(down, self.step)
            self.put(up, -self.step)
        else:
            self.put(up, far)
            self.put(down, far, half)
            self.over = True
        self.step += 1
        return others


class ReduceRun:
    def __init__(self, ring, order, part):
        self.ring, self.order, self.part = ring, order, part
        far = part(ring.n // 2)
        (far,) = order.gate(far)
        self.half = far.shape[0] // 2
        self.up, self.down = ring.up(far[: self.half]), ring.down(far[self.half :])
        self.step, self.over = ring.n // 2 - 1, False

    def turn(self, others):
        half = self.half
        up, down, *others = self.order.gate(self.up, self.down, *others)
        up, down = up.astype(F32), down.astype(F32)
        if self.step == 0:
            self.result = self.part(0).astype(F32) + up + down
            self.over = True
            return others
        a, b = self.part(self.step), self.part(-self.step)
        if self.step == self.ring.n // 2 - 1:
            a = lax.dynamic_update_slice(a, (a[:half].astype(F32) + up).astype(BF16), (0, 0))
            b = lax.dynamic_update_slice(b, (b[half:].astype(F32) + down).astype(BF16), (half, 0))
        else:
            a = (a.astype(F32) + up).astype(BF16)
            b = (b.astype(F32) + down).astype(BF16)
        self.up, self.down = self.ring.up(a), self.ring.down(b)
        self.step -= 1
        return others


def sum_everywhere(value, batch):
    value = value + core_swap(value)
    value = value + y_swap(value)
    bit = 1
    while bit < batch:
        value = value + lax.ppermute(value, "batch", [(i, i ^ bit) for i in range(batch)])
        bit *= 2
    return value


class Spread:
    def __init__(self, parts, j):
        self.parts, self.j = parts, j
        self.got = y_swap(jnp.stack([parts[j ^ 2], parts[j ^ 3]]))

    def cross(self):
        self.across = core_swap(jnp.stack([self.parts[self.j ^ 1], self.got[1]]))

    def block(self):
        blocks = [self.parts[self.j], self.across[0], self.got[0], self.across[1]]
        whole = absolute(blocks, self.j)
        return whole.reshape(NC * whole.shape[1], whole.shape[2])


class Collect:
    def __init__(self, block, j):
        self.block, self.j = block, j
        self.got = core_swap(jnp.stack([block[j ^ 1], block[j ^ 3]]))

    def cross(self):
        self.far = y_swap(jnp.stack([self.block[self.j ^ 2], self.got[1]]))

    def result(self):
        whole = absolute([self.block[self.j], self.got[0], self.far[0], self.far[1]], self.j)
        return whole.astype(F32)


def absolute(blocks, j):
    whole = jnp.zeros((NC,) + blocks[0].shape, blocks[0].dtype)
    for k in range(NC):
        whole = lax.dynamic_update_slice(
            whole, blocks[k][None], (j ^ k,) + (0,) * blocks[0].ndim
        )
    return whole


def stacked(blocks):
    size = blocks[0].shape[0]
    whole = jnp.zeros((len(blocks) * size,) + blocks[0].shape[1:], blocks[0].dtype)
    for k, block in enumerate(blocks):
        whole = lax.dynamic_update_slice_in_dim(whole, block, k * size, 0)
    return whole


class Near:
    def __init__(self, own):
        self.own, self.far, self.next = own, y_swap(own), core_swap(own)

    def cross(self):
        self.last = core_swap(self.far)

    def blocks(self):
        return [self.own, self.next, self.far, self.last]


class NearSum:
    def __init__(self, part, at, between=None):
        self.part, self.at = part, at
        self.away = part(True)
        self.third = core_swap(self.away[1 - at].astype(BF16))
        if between is None:
            self.go()
            self.stay()

    def go(self):
        self.second = y_swap((self.away[self.at] + self.third.astype(F32)).astype(BF16))

    def stay(self):
        home = self.part(False)
        self.first = core_swap(home[1 - self.at].astype(BF16))
        self.near = home[self.at]

    def result(self):
        return self.near + self.first.astype(F32) + self.second.astype(F32)


PAIR = 2 * P_SIZE
EDGE = 8


def halves(first, second, lanes):
    return jnp.where(lanes < P_SIZE, first, second)


def step_values(raw, bias, log, marks):
    rows = lax.broadcasted_iota(jnp.int32, (CHUNK, CHUNK), 0)
    cols = lax.broadcasted_iota(jnp.int32, (CHUNK, CHUNK), 1)
    value = raw + bias
    step = jnp.maximum(value, 0.0) + jnp.log1p(jnp.exp(-jnp.abs(value)))
    decay = -jnp.exp(log) * step
    lower = (rows >= cols).astype(F32)
    cum = jnp.dot(lower, decay, precision=HIGHEST, preferred_element_type=F32)
    end = cum[CHUNK - 1 :, :]
    seg, before, last = marks[:, 0:1], marks[:, 1:2], marks[:, 2:3]
    reach = jnp.where(seg == before, jnp.exp(cum), 0.0)
    bare = jnp.where(seg == last, jnp.exp(end - cum), 0.0)
    through = jnp.where(last[:1] == before[:1], jnp.exp(end), 0.0)
    return value, step, decay, cum, reach, bare, through


def convolved(buf, taps, marks, width):
    total = taps[0:1, :width] * buf[EDGE : EDGE + CHUNK, :width]
    for lag in range(1, TAPS):
        moved = buf[EDGE - lag : EDGE - lag + CHUNK, :width]
        total = total + taps[lag : lag + 1, :width] * moved * marks[:, 2 + lag : 3 + lag]
    return total


def ssd_forward_kernel(
    x_ref, bc_ref, raw_ref, bias_ref, log_ref, taps_ref, tapsb_ref, mark_ref, row_ref, skip_ref,
    y_ref, st_ref, conv_ref, act_ref, step_ref, reach_ref, bare_ref, cum_ref, cumt_ref, end_ref,
    state, buf, bufb
):
    @pl.when(pl.program_id(0) == 0)
    def _():
        state[...] = jnp.zeros_like(state)
        buf[...] = jnp.zeros_like(buf)
        bufb[...] = jnp.zeros_like(bufb)

    marks = mark_ref[...]
    for b_, ref in ((buf, x_ref), (bufb, bc_ref)):
        b_[0:EDGE, :] = b_[CHUNK : CHUNK + EDGE, :]
        b_[EDGE : EDGE + CHUNK, :] = ref[...].astype(F32)
    conv = convolved(bufb, tapsb_ref, marks, 2 * N)
    bc = (conv * jax.nn.sigmoid(conv)).astype(BF16)
    act_ref[...] = bc
    b, c = bc[:, :N], bc[:, N:]
    _, step, _, cum, reach, bare, through = step_values(
        raw_ref[...], bias_ref[...], log_ref[...], marks
    )
    weight = bare * step
    cum_rows = cum.T
    step_ref[...], reach_ref[...], bare_ref[...], cum_ref[...] = step, reach, bare, cum
    cumt_ref[...] = cum_rows[:16, :]
    end_ref[...] = jnp.broadcast_to(through, (8, 128))
    rows = lax.broadcasted_iota(jnp.int32, (CHUNK, CHUNK), 0)
    cols = lax.broadcasted_iota(jnp.int32, (CHUNK, CHUNK), 1)
    allowed = (marks[:, 0:1] == row_ref[0:1, :]) & (rows >= cols)
    inner = mm_nt(c, b)
    lanes = lax.broadcasted_iota(jnp.int32, (CHUNK, PAIR), 1)
    subs = lax.broadcasted_iota(jnp.int32, (PAIR, N), 0)
    spans = [slice(PAIR * p, PAIR * (p + 1)) for p in range(PAIRS)]

    def picked(value):
        return [
            halves(value[:, 2 * p : 2 * p + 1], value[:, 2 * p + 1 : 2 * p + 2], lanes)
            for p in range(PAIRS)
        ]

    held = [state[span, :] for span in spans]
    low = [v.astype(BF16) for v in held]
    carried = [mm_nt(c, v) for v in low]
    x = []
    for span in spans:
        conv = taps_ref[0:1, span] * buf[EDGE : EDGE + CHUNK, span]
        for lag in range(1, TAPS):
            moved = buf[EDGE - lag : EDGE - lag + CHUNK, span]
            conv = conv + taps_ref[lag : lag + 1, span] * moved * marks[:, 2 + lag : 3 + lag]
        conv_ref[:, span] = conv
        x.append(conv * jax.nn.sigmoid(conv))
    scaled = [(v * w).astype(BF16) for v, w in zip(x, picked(step))]
    weighed = [(v * w).astype(BF16) for v, w in zip(x, picked(weight))]
    tails = [mm_tn(v, b) for v in weighed]
    mixing = []
    for q in range(HEADS):
        spread = cum[:, q : q + 1] - cum_rows[q : q + 1, :]
        mixing.append((jnp.exp(jnp.where(allowed, spread, -1e30)) * inner).astype(BF16))
    local = [mm(mixing[q], scaled[q // 2]) for q in range(HEADS)]
    reach2 = picked(reach)
    for p, span in enumerate(spans):
        st_ref[0, span, :] = low[p]
        y_ref[:, span] = (
            halves(local[2 * p], local[2 * p + 1], lanes)
            + reach2[p] * carried[p]
            + skip_ref[:, span] * x[p]
        )
        kept = jnp.where(subs < P_SIZE, through[:, 2 * p : 2 * p + 1], through[:, 2 * p + 1 : 2 * p + 2])
        state[span, :] = kept * held[p] + tails[p]


def ssd_backward_kernel(first, *refs):
    (g_ref, x_ref, xp_ref, conv_ref, act_ref, step_ref, reach_ref, bare_ref), refs = refs[:8], refs[8:]
    (cum_ref, cumt_ref, end_ref, st_ref, raw_ref, bias_ref, log_ref), refs = refs[:7], refs[7:]
    (taps_ref, _, mark_ref, row_ref, skip_ref), refs = refs[:5], refs[5:]
    if first:
        (dbc_in, draw_in, _), refs = refs[:3], refs[3:]
    dx_ref, dbc_ref, draw_ref, sums_ref, tsums_ref, later, buf, ahead_buf = refs

    @pl.when(pl.program_id(0) == 0)
    def _():
        later[...] = jnp.zeros_like(later)
        sums_ref[...] = jnp.zeros_like(sums_ref)
        tsums_ref[...] = jnp.zeros_like(tsums_ref)
        ahead_buf[...] = jnp.zeros_like(ahead_buf)

    marks = mark_ref[...]
    buf[0:EDGE, :] = xp_ref[CHUNK - 2 * EDGE :, :].astype(F32)[EDGE:, :]
    buf[EDGE : EDGE + CHUNK, :] = x_ref[...].astype(F32)
    b, c = act_ref[:, :N], act_ref[:, N:]
    step, reach, bare, cum = step_ref[...], reach_ref[...], bare_ref[...], cum_ref[...]
    cum_rows, through = cumt_ref[...], end_ref[0:1, :]
    weight = bare * step
    rows = lax.broadcasted_iota(jnp.int32, (CHUNK, CHUNK), 0)
    cols = lax.broadcasted_iota(jnp.int32, (CHUNK, CHUNK), 1)
    allowed = (marks[:, 0:1] == row_ref[0:1, :]) & (rows >= cols)
    inner = mm_nt(c, b)
    lanes = lax.broadcasted_iota(jnp.int32, (CHUNK, PAIR), 1)
    subs = lax.broadcasted_iota(jnp.int32, (PAIR, N), 0)
    wide = lax.broadcasted_iota(jnp.int32, (CHUNK, 128), 1)
    last = lax.broadcasted_iota(jnp.int32, (CHUNK, 1), 0) == CHUNK - 1
    d_inner = jnp.zeros((CHUNK, CHUNK), F32)
    db = jnp.zeros((CHUNK, N), F32)
    dc = jnp.zeros((CHUNK, N), F32)
    d_cum = jnp.zeros((CHUNK, 128), F32)
    d_step = jnp.zeros((CHUNK, 128), F32)
    ahead_buf[CHUNK : CHUNK + EDGE, :] = ahead_buf[0:EDGE, :]
    count = range(PAIRS // 2)
    spans = [slice(PAIR * p, PAIR * (p + 1)) for p in count]

    def picked(value):
        return [
            halves(value[:, h : h + 1], value[:, h + 1 : h + 2], lanes)
            for h in (2 * (p + first) for p in count)
        ]

    conv = [conv_ref[:, span] for span in spans]
    g = [g_ref[:, span] for span in spans]
    start = [st_ref[0, span, :] for span in spans]
    ahead = [later[span, :].astype(BF16) for span in spans]
    bs = [mm_nt(b, a) for a in ahead]
    cs = [mm_nt(c, a) for a in start]
    sg = [jax.nn.sigmoid(v) for v in conv]
    x = [v * w for v, w in zip(conv, sg)]
    step2, reach2, weight2, bare2 = picked(step), picked(reach), picked(weight), picked(bare)
    scaled = [(v * w).astype(BF16) for v, w in zip(x, step2)]
    e = []
    for q in range(PAIRS):
        spread = cum[:, 2 * first + q : 2 * first + q + 1] - cum_rows[2 * first + q : 2 * first + q + 1, :]
        e.append(jnp.exp(jnp.where(allowed, spread, -1e30)))
    d_mix = []
    for p in count:
        for q in (0, 1):
            mine = (lanes >= P_SIZE) if q else (lanes < P_SIZE)
            d_mix.append(mm_nt(jnp.where(mine, g[p], 0.0).astype(BF16), scaled[p]))
    mixing = [v * inner for v in e]
    local = [mm_tn(mixing[q].astype(BF16), g[q // 2].astype(BF16)) for q in range(PAIRS)]
    totals = []
    for q in range(PAIRS):
        d_inner = d_inner + d_mix[q] * e[q]
        totals.append(jnp.sum(d_mix[q] * mixing[q], axis=1, keepdims=True))
    local = [halves(local[2 * p], local[2 * p + 1], lanes) for p in count]
    gr = [(v * w).astype(BF16) for v, w in zip(reach2, g)]
    wx = [(v * w).astype(BF16) for v, w in zip(weight2, x)]
    for p in count:
        dc = dc + mm(gr[p], start[p])
        db = db + mm(wx[p], ahead[p])
    for p in count:
        h = 2 * (p + first)
        held = later[spans[p], :]
        product = held * start[p].astype(F32)
        kept = jnp.where(subs < P_SIZE, through[:, h : h + 1], through[:, h + 1 : h + 2])
        later[spans[p], :] = kept * held + mm_tn(gr[p], c)
        xbs = x[p] * bs[p]
        xl = x[p] * local[p]
        stored = xbs * weight2[p]
        direct = xbs * bare2[p] + xl
        change = g[p] * cs[p] * reach2[p] - stored - xl * step2[p]
        for q in (0, 1):
            mine = (lanes >= P_SIZE) if q else (lanes < P_SIZE)
            half = slice(P_SIZE * q, P_SIZE * (q + 1))
            stored_sum = jnp.sum(jnp.sum(stored, axis=0, keepdims=True)[:, half], keepdims=True)
            held_sum = jnp.sum(jnp.sum(product[half], axis=0, keepdims=True), keepdims=True)
            end = stored_sum + through[:, h + q : h + q + 1] * held_sum
            cum_q = totals[2 * p + q] + jnp.sum(jnp.where(mine, change, 0.0), axis=1, keepdims=True)
            cum_q = cum_q + jnp.where(last, end, 0.0)
            step_q = jnp.sum(jnp.where(mine, direct, 0.0), axis=1, keepdims=True)
            d_cum = jnp.where(wide == h + q, cum_q, d_cum)
            d_step = jnp.where(wide == h + q, step_q, d_step)
    d_conv = []
    for p in count:
        span = spans[p]
        dx = local[p] * step2[p] + weight2[p] * bs[p] + skip_ref[:, span] * g[p]
        d_conv.append(dx * sg[p] * (1.0 + conv[p] * (1.0 - sg[p])))
        ahead_buf[0:CHUNK, span] = d_conv[p]
    for p in count:
        span = spans[p]
        d_in = taps_ref[0:1, span] * d_conv[p]
        for lag in range(1, TAPS):
            d_in = d_in + taps_ref[lag : lag + 1, span] * (
                ahead_buf[lag : lag + CHUNK, span] * marks[:, 5 + lag : 6 + lag]
            )
        dx_ref[:, span] = d_in.astype(BF16)
        for lag in range(TAPS):
            moved = buf[EDGE - lag : EDGE - lag + CHUNK, span]
            if lag:
                moved = moved * marks[:, 2 + lag : 3 + lag]
            tsums_ref[lag : lag + 1, span] += jnp.sum(d_conv[p] * moved, axis=0, keepdims=True)
        tsums_ref[TAPS : TAPS + 1, span] += jnp.sum(g[p] * x[p], axis=0, keepdims=True)
    di = d_inner.astype(BF16)
    db = db + mm_tn(di, c)
    dc = dc + mm(di, b)
    for q, part in enumerate((db[:, :WB], db[:, WB:], dc[:, :WB], dc[:, WB:])):
        dbc_ref[q] = part + dbc_in[q] if first else part
    upper = (cols >= rows).astype(F32)
    d_decay = jnp.dot(upper, d_cum, precision=HIGHEST, preferred_element_type=F32)
    rate = jnp.exp(log_ref[...])
    d_raw = (d_step - rate * d_decay) * jax.nn.sigmoid(raw_ref[...] + bias_ref[...])
    sums_ref[0:1, :] += jnp.sum(d_raw, axis=0, keepdims=True)
    sums_ref[1:2, :] -= jnp.sum(d_decay * (rate * step), axis=0, keepdims=True)
    draw_ref[...] = d_raw + draw_in[...] if first else d_raw


def ssd_specs(chunks, flip, width, part):
    def at(i):
        return chunks - 1 - i if flip else i

    def rowwise(size, col=0):
        return pl.BlockSpec((CHUNK, size), lambda i: (at(i), col))

    def fixed(height, size, col=0):
        return pl.BlockSpec((height, size), lambda i: (0, col))

    def behind(size, col=0):
        return pl.BlockSpec((CHUNK, size), lambda i: (jnp.maximum(at(i) - 1, 0), col))

    def across(height):
        return pl.BlockSpec((height, CHUNK), lambda i: (0, at(i)))

    states = pl.BlockSpec((1, width, N), lambda i: (at(i), part, 0))
    dbc = pl.BlockSpec((NC, CHUNK, WB), lambda i: (0, at(i), 0))
    end = pl.BlockSpec((8, 128), lambda i: (at(i), 0))
    kept = [rowwise(width, part), rowwise(2 * N)] + [rowwise(128)] * 4 + [across(16), end]
    tail = [
        rowwise(128), fixed(1, 128), fixed(1, 128), fixed(TAPS, width, part), fixed(TAPS, 2 * N),
        rowwise(16), across(8), fixed(1, width, part),
    ]
    return rowwise, fixed, behind, states, dbc, kept, tail


def ssd_forward(x, bc, *rest):
    tokens = x.shape[0]
    chunks = tokens // CHUNK
    rowwise, _, _, states, _, kept, tail = ssd_specs(chunks, False, WX, 0)
    by_token = jax.ShapeDtypeStruct((tokens, 128), F32)
    y, states, *saved = pl.pallas_call(
        ssd_forward_kernel,
        grid=(chunks,),
        in_specs=[rowwise(WX), rowwise(2 * N)] + tail,
        out_specs=[rowwise(WX), states] + kept,
        out_shape=[
            jax.ShapeDtypeStruct((tokens, WX), F32),
            jax.ShapeDtypeStruct((chunks, WX, N), BF16),
            jax.ShapeDtypeStruct((tokens, WX), F32),
            jax.ShapeDtypeStruct((tokens, 2 * N), BF16),
            by_token,
            by_token,
            by_token,
            by_token,
            jax.ShapeDtypeStruct((16, tokens), F32),
            jax.ShapeDtypeStruct((8 * chunks, 128), F32),
        ],
        scratch_shapes=[
            pltpu.VMEM((WX, N), F32),
            pltpu.VMEM((CHUNK + EDGE, WX), F32),
            pltpu.VMEM((CHUNK + EDGE, 2 * N), F32),
        ],
        compiler_params=pltpu.CompilerParams(
            dimension_semantics=("arbitrary",), vmem_limit_bytes=40 << 20
        ),
        name="ssd_forward",
    )(x, bc, *rest)
    return y, (*saved, states)


def ssd_backward(part, g, x, saved, rest, earlier=()):
    tokens = x.shape[0]
    chunks = tokens // CHUNK
    half = WX // 2
    rowwise, fixed, behind, st, dbc, kept, tail = ssd_specs(chunks, True, half, part)
    extra = [dbc, rowwise(128), pl.BlockSpec(memory_space=pl.ANY)] if part else []
    return pl.pallas_call(
        functools.partial(ssd_backward_kernel, part * PAIRS // 2),
        grid=(chunks,),
        in_specs=[rowwise(half, part), rowwise(half, part), behind(half, part)]
        + kept
        + [st]
        + tail
        + extra,
        out_specs=[rowwise(half, part), dbc, rowwise(128), fixed(8, 128), fixed(8, half)],
        out_shape=[
            jax.ShapeDtypeStruct((tokens, WX), BF16),
            jax.ShapeDtypeStruct((NC, tokens, WB), F32),
            jax.ShapeDtypeStruct((tokens, 128), F32),
            jax.ShapeDtypeStruct((8, 128), F32),
            jax.ShapeDtypeStruct((8, half), F32),
        ],
        scratch_shapes=[
            pltpu.VMEM((half, N), F32),
            pltpu.VMEM((CHUNK + EDGE, half), F32),
            pltpu.VMEM((CHUNK + EDGE, half), F32),
        ],
        input_output_aliases={22: 0} if part else {},
        compiler_params=pltpu.CompilerParams(
            dimension_semantics=("arbitrary",), vmem_limit_bytes=40 << 20
        ),
        name="ssd_backward",
    )(g, x, x, *saved, *rest, *earlier)


Q_BLOCK = 256
SCALE = HEAD_SIZE ** (-0.5)


def attention_probs(q, k, segc, segr, i):
    scores = mm_nt(q, k) * SCALE
    rows = lax.broadcasted_iota(jnp.int32, scores.shape, 0) + i * Q_BLOCK
    cols = lax.broadcasted_iota(jnp.int32, scores.shape, 1)
    scores = jnp.where((rows >= cols) & (segc == segr), scores, -1e30)
    grown = jnp.exp(scores - jnp.max(scores, axis=-1, keepdims=True))
    return grown / jnp.sum(grown, axis=-1, keepdims=True)


def attention_forward_kernel(q_ref, k_ref, v_ref, segc_ref, segr_ref, o_ref):
    for i in range(k_ref.shape[0] // Q_BLOCK):

        @pl.when(pl.program_id(1) == i)
        def _():
            seen = slice(0, (i + 1) * Q_BLOCK)
            probs = attention_probs(q_ref[...], k_ref[seen, :], segc_ref[...], segr_ref[:, seen], i)
            o_ref[...] = mm(probs.astype(BF16), v_ref[seen, :]).astype(BF16)


def attention_backward_kernel(
    q_ref, k_ref, v_ref, segc_ref, segr_ref, g_ref, dq_ref, dk_ref, dv_ref
):
    @pl.when((pl.program_id(0) == 0) & (pl.program_id(1) == 0))
    def _():
        dk_ref[...] = jnp.zeros_like(dk_ref)
        dv_ref[...] = jnp.zeros_like(dv_ref)

    for i in range(k_ref.shape[0] // Q_BLOCK):

        @pl.when(pl.program_id(1) == i)
        def _():
            seen = slice(0, (i + 1) * Q_BLOCK)
            q, k, g = q_ref[...], k_ref[seen, :], g_ref[...]
            probs = attention_probs(q, k, segc_ref[...], segr_ref[:, seen], i)
            d_probs = mm_nt(g, v_ref[seen, :])
            inner = jnp.sum(probs * d_probs, axis=-1, keepdims=True)
            d_scores = (probs * (d_probs - inner)).astype(BF16)
            dq_ref[...] = mm(d_scores, k) * SCALE
            dk_ref[seen, :] += mm_tn(d_scores, q) * SCALE
            dv_ref[seen, :] += mm_tn(probs.astype(BF16), g)


def attention_specs(tokens):
    block = pl.BlockSpec((Q_BLOCK, HEAD_SIZE), lambda h, i: (i, h))
    whole = pl.BlockSpec((tokens, HEAD_SIZE), lambda h, i: (0, 0))
    segc = pl.BlockSpec((Q_BLOCK, 1), lambda h, i: (i, 0))
    segr = pl.BlockSpec((1, tokens), lambda h, i: (0, 0))
    params = pltpu.CompilerParams(
        dimension_semantics=("arbitrary", "arbitrary"), vmem_limit_bytes=32 << 20
    )
    return block, whole, segc, segr, params


def attention_forward(q, k, v, segc, segr):
    tokens = q.shape[0]
    block, whole, sc, sr, params = attention_specs(tokens)
    return pl.pallas_call(
        attention_forward_kernel,
        grid=(QH, tokens // Q_BLOCK),
        in_specs=[block, whole, whole, sc, sr],
        out_specs=block,
        out_shape=jax.ShapeDtypeStruct((tokens, QH * HEAD_SIZE), BF16),
        compiler_params=params,
        name="attention_forward",
    )(q, k, v, segc, segr)


def attention_backward(q, k, v, segc, segr, g):
    tokens = q.shape[0]
    block, whole, sc, sr, params = attention_specs(tokens)
    return pl.pallas_call(
        attention_backward_kernel,
        grid=(QH, tokens // Q_BLOCK),
        in_specs=[block, whole, whole, sc, sr, block],
        out_specs=[block, whole, whole],
        out_shape=[
            jax.ShapeDtypeStruct((tokens, QH * HEAD_SIZE), F32),
            jax.ShapeDtypeStruct((tokens, HEAD_SIZE), F32),
            jax.ShapeDtypeStruct((tokens, HEAD_SIZE), F32),
        ],
        compiler_params=params,
        name="attention_backward",
    )(q, k, v, segc, segr, g)


def rms_of(rows):
    return lax.rsqrt(jnp.mean(rows * rows, axis=-1, keepdims=True) + NORM_EPSILON)


def norm_back(grad, rows, r, gain):
    w = grad * gain
    return r * w - rows * (r * r * r) * jnp.mean(w * rows, axis=-1, keepdims=True)


def silu_slope(value):
    sg = jax.nn.sigmoid(value)
    return sg * (1.0 + value * (1.0 - sg))


def turned(heads, cosine, sine):
    half = HEAD_SIZE // 2
    parts = []
    for h in range(heads.shape[1] // HEAD_SIZE):
        v = heads[:, h * HEAD_SIZE : (h + 1) * HEAD_SIZE]
        parts.append(v * cosine + jnp.concatenate([v[:, half:], v[:, :half]], axis=1) * sine)
    return jnp.concatenate(parts, axis=1)


def shifted(value, lag):
    if lag == 0:
        return value
    zeros = jnp.zeros((abs(lag), value.shape[1]), value.dtype)
    if lag > 0:
        return jnp.concatenate([zeros, value[:-lag]], axis=0)
    return jnp.concatenate([value[-lag:], zeros], axis=0)


def convolve(value, taps, keeps):
    total = taps[0][None] * value
    for lag in range(1, TAPS):
        total = total + taps[lag][None] * shifted(value, lag) * keeps[lag]
    return total


def body(
    tokens,
    segment_ids,
    valid_mask,
    teacher,
    mixer_in,
    mixer_out,
    query_weight,
    key_value_weight,
    output_weight,
    gate_up,
    down_weight,
    norm_first,
    norm_second,
    conv_taps,
    decay_log,
    skip_gain,
    step_bias,
):
    ring = Ring()
    nb = ring.n
    j = lax.axis_index("ctx")
    own = tokens.shape[0] * tokens.shape[1]
    length = own * NC
    devices = nb * NC
    total_tokens = float(own * devices)
    x = tokens.reshape(own, MODEL_WIDTH).astype(F32)
    valid = valid_mask.reshape(own).astype(F32)
    target = teacher.reshape(own, MODEL_WIDTH).astype(F32)

    order = Order(jnp.broadcast_to(valid[:1] * 0.0, (8, 128)))
    gate, scale = order.gate, max(1, nb // 8)

    def turn(run, *others):
        for _ in range(scale):
            if not run.over:
                others = run.turn(others)
        return others[0] if len(others) == 1 else others

    def finish(run, *others):
        while not run.over:
            others = run.turn(others)
        return others[0] if len(others) == 1 else others

    def start(block, place=lambda b: b):
        return GatherRun(ring, order, block, place)

    rows = mixer_in.shape[0]
    edge = 2 * DI + 2 * N
    unit = down_weight.shape[0]
    near_seg = Near(segment_ids.reshape(1, own))
    g_down = start(down_weight)
    rows_out, rows_attn = mixer_out.shape[0], output_weight.shape[0]

    def home(q):
        return (q % 2) * 4 + q // 2 % 2 * 2 + q // 4 if nb == 8 else q

    there = [(m, home(m % nb) * NC + m // nb) for m in range(devices)]
    back = [(b, a) for a, b in there]
    both_out = lax.ppermute(
        jnp.concatenate([mixer_out, output_weight], axis=0), ("batch", "ctx"), there
    )
    xs_cols = mixer_in[:, DI : 2 * DI].reshape(rows, NC, WX)
    bc_cols = mixer_in[:, 2 * DI : edge].reshape(rows, NC, WB)
    dt_cols = mixer_in[:, edge:].reshape(rows, NC, HEADS)
    digits = jnp.sum(valid)
    digits = jnp.stack([jnp.floor(digits / 64.0), digits % 64.0]).astype(BF16)
    shape = (rows, NC, 128 - HEADS)
    lane = lax.broadcasted_iota(jnp.int32, shape, 2) - (126 - HEADS)
    lane = jnp.where(lax.broadcasted_iota(jnp.int32, shape, 0) == 0, lane, -1)
    padding = jnp.where(lane == 0, digits[0], jnp.where(lane == 1, digits[1], 0))
    dt_cols = jnp.concatenate([dt_cols, padding.astype(BF16)], axis=2)
    first_cols = jnp.concatenate([xs_cols, bc_cols, dt_cols], axis=2).transpose(1, 0, 2)
    spread = Spread(first_cols, j)
    spread.got, mixer_in, query_weight, key_value_weight, x, near_seg.far, near_seg.next = turn(
        g_down, spread.got, mixer_in, query_weight, key_value_weight, x, near_seg.far,
        near_seg.next
    )
    spread.cross()
    near_seg.cross()
    z_cols = mixer_in[:, :DI].reshape(rows, NC, WX)
    q_cols = query_weight.reshape(rows, NC, WQ)
    kv = key_value_weight.reshape(rows, 2, 2, HEAD_SIZE)
    kv_cols = kv.transpose(0, 2, 1, 3).reshape(rows, NC, HEAD_SIZE)
    second_cols = jnp.concatenate([q_cols, kv_cols, z_cols], axis=2).transpose(1, 0, 2)
    spread_two = Spread(second_cols, j)
    (spread.across, x) = gate(spread.across, x)
    g_first = start(spread.block())
    r_x = rms_of(x)
    normed_own = (x * r_x * norm_first).astype(BF16)
    near_normed = Near(normed_own)
    spread_two.got, near_normed.next = turn(g_down, spread_two.got, near_normed.next)
    spread_two.cross()
    gate_up, both_out = turn(g_first, gate_up, both_out)
    spread_two.across = turn(g_down, spread_two.across)
    gu_cols = (
        gate_up.reshape(rows, 2, nb, NC, unit).transpose(3, 0, 1, 2, 4).reshape(NC, rows, 2 * WF)
    )
    spread_gu = Spread(gu_cols, j)
    near_normed.far, near_seg.last = turn(g_first, near_normed.far, near_seg.last)
    near_normed.cross()
    g_second = start(spread_two.block())
    place = jnp.arange(length, dtype=jnp.int32)
    near_normed.last, conv_taps, decay_log, skip_gain, step_bias, place = finish(
        g_down, near_normed.last, conv_taps, decay_log, skip_gain, step_bias, place
    )
    normed = absolute(near_normed.blocks(), j).reshape(length, MODEL_WIDTH)
    w_down = g_down.whole

    seg = absolute(near_seg.blocks(), j).reshape(length)
    keeps, marks_ahead = [None], []
    for lag in range(1, TAPS):
        before = jnp.concatenate([jnp.full((lag,), -1, jnp.int32), seg[:-lag]])
        after_it = jnp.concatenate([seg[lag:], jnp.full((lag,), -1, jnp.int32)])
        keeps.append((before == seg).astype(F32))
        marks_ahead.append((after_it == seg).astype(F32))
    chunks = length // CHUNK
    seg_f = seg.astype(F32)
    seg_last = seg_f.reshape(chunks, CHUNK)[:, -1]
    seg_prev = jnp.concatenate([jnp.full((1,), -1.0, F32), seg_last[:-1]])
    marks = jnp.stack(
        [seg_f, jnp.repeat(seg_prev, CHUNK), jnp.repeat(seg_last, CHUNK)] + keeps[1:] + marks_ahead
        + [jnp.zeros_like(seg_f)] * 7
    ).T
    row = jnp.broadcast_to(seg_f[None, :], (8, length))
    keeps = [None] + [marks[:, 2 + lag : 3 + lag] for lag in range(1, TAPS)]
    marks, row, spread_gu.got = turn(g_first, marks, row, spread_gu.got)
    spread_gu.cross()
    half = HEAD_SIZE // 2
    inverse = ROPE_BASE ** (-(jnp.arange(half, dtype=F32) * 2.0) / HEAD_SIZE)
    angle = place.astype(F32)[:, None] * inverse[None, :]
    cosine, sine = jnp.cos(angle), jnp.sin(angle)
    cosine = jnp.concatenate([cosine, cosine], axis=1)
    sine = jnp.concatenate([-sine, sine], axis=1)
    heads_at = j * HEADS
    lane_pad = ((0, 0), (0, 128 - HEADS))
    own_log = jnp.pad(lax.dynamic_slice_in_dim(decay_log, heads_at, HEADS)[None], lane_pad)
    own_bias = jnp.pad(lax.dynamic_slice_in_dim(step_bias, heads_at, HEADS)[None], lane_pad)
    own_skip = lax.dynamic_slice_in_dim(skip_gain, heads_at, HEADS)
    skip_wide = jnp.repeat(own_skip, P_SIZE)[None, :]
    taps_x = lax.dynamic_slice(conv_taps, (0, j * WX), (TAPS, WX))
    taps_b = conv_taps[:, DI:]
    taps_b_own = lax.dynamic_slice(conv_taps, (0, DI + j * WB), (TAPS, WB))
    cosine, sine, normed = finish(g_first, cosine, sine, normed)
    w_first = g_first.whole
    digits = jnp.sum(w_first[::rows, -2:].astype(F32), axis=0)
    count = digits[0] * 64.0 + digits[1]
    lane = jnp.arange(128)[None, :]
    w_raw = jnp.where(lane < HEADS, w_first[:, WX + WB :], 0)

    conv_b_own = mm(normed, w_first[:, WX : WX + WB]).astype(BF16)
    b_far = y_swap(conv_b_own)
    conv_b_own, normed, w_first = turn(g_second, conv_b_own, normed, w_first)
    step_raw = mm(normed, w_raw)
    conv_x = mm(normed, w_first[:, :WX]).astype(BF16)
    conv_x, step_raw, b_far = turn(g_second, conv_x, step_raw, b_far)
    b_other = core_swap(jnp.concatenate([conv_b_own, b_far], axis=1))
    g_out = start(both_out, lambda b: home(b))
    upper, core = j // 2, j % 2
    mine = (jnp.where(upper == 0, conv_b_own, b_far), jnp.where(upper == 0, b_far, conv_b_own))
    (b_other,) = gate(b_other)
    theirs = (
        jnp.where(upper == 0, b_other[:, :WB], b_other[:, WB:]),
        jnp.where(upper == 0, b_other[:, WB:], b_other[:, :WB]),
    )
    conv_b = jnp.concatenate(
        [
            jnp.where(core == 0, mine[0], theirs[0]),
            jnp.where(core == 0, theirs[0], mine[0]),
            jnp.where(core == 0, mine[1], theirs[1]),
            jnp.where(core == 0, theirs[1], mine[1]),
        ],
        axis=1,
    )
    rest_ssd = (step_raw, own_bias, own_log, taps_x, taps_b, marks, row, skip_wide)
    ssm_y, saved = ssd_forward(conv_x, conv_b, *rest_ssd)
    ssm_y, normed = turn(g_second, ssm_y, normed)
    ssm_y, normed = turn(g_out, ssm_y, normed)
    normed, spread_gu.across = finish(g_second, normed, spread_gu.across)
    w_second = g_second.whole
    rest = mm(normed, w_second)
    rest = turn(g_out, rest)
    gate_z = rest[:, WQ + HEAD_SIZE :]
    queries = turned(rest[:, :WQ], cosine, sine).astype(BF16)
    kv_raw = rest[:, WQ : WQ + HEAD_SIZE]
    kv_own = jnp.where(core == 0, turned(kv_raw, cosine, sine), kv_raw).astype(BF16)
    kv_other = core_swap(kv_own)
    queries, kv_own, kv_other, gate_z = turn(g_out, queries, kv_own, kv_other, gate_z)
    g_gu = start(spread_gu.block())
    keys = jnp.where(core == 0, kv_own, kv_other)
    values = jnp.where(core == 0, kv_other, kv_own)
    segc, segr = seg[:, None], seg[None, :]
    attended = attention_forward(queries, keys, values, segc, segr)
    silu_z = jax.nn.silu(gate_z)
    gated = (ssm_y * silu_z).astype(BF16)
    attended, gated = turn(g_out, attended, gated)
    acts = jnp.concatenate([gated, attended], axis=1)
    acts = finish(g_out, acts)
    out_all = g_out.whole.reshape(nb, rows_out + rows_attn, MODEL_WIDTH)
    w_out = jnp.concatenate(
        [
            out_all[:, :rows_out].reshape(WX, MODEL_WIDTH),
            out_all[:, rows_out:].reshape(WQ, MODEL_WIDTH),
        ],
        axis=0,
    )


    def upper_rows(value, far):
        return lax.dynamic_slice_in_dim(value, (1 - upper if far else upper) * 2 * own, 2 * own)

    def in_two(value):
        return value.reshape(2, own, -1)

    mixed = NearSum(lambda far: in_two(mm(upper_rows(acts, far), w_out)), core)
    mixed.first, mixed.near = turn(g_gu, mixed.first, mixed.near)
    (mixed.second,) = gate(mixed.second)
    hidden_one = x + mixed.result()
    r_h = rms_of(hidden_one)
    normed_two_own = (hidden_one * r_h * norm_second).astype(BF16)
    (normed_two_own,) = gate(normed_two_own)
    near_two = Near(normed_two_own)
    near_two.next = turn(g_gu, near_two.next)
    near_two.far = turn(g_gu, near_two.far)
    near_two.cross()
    normed_two = near_two.blocks()
    normed_two_all = stacked(normed_two)
    normed_two = list(finish(g_gu, *normed_two))
    w_gu = g_gu.whole

    (normed_two_all,) = gate(normed_two_all)
    gateup = mm(normed_two_all, w_gu)
    hidden_all = (jax.nn.silu(gateup[:, :WF]) * gateup[:, WF:]).astype(BF16)

    def near_rows(value, far):
        return value[2 * own :] if far else value[: 2 * own]

    ffn = NearSum(lambda far: in_two(mm(near_rows(hidden_all, far), w_down)), 0)
    (ffn.second,) = gate(ffn.second)
    final = hidden_one + ffn.result()
    error = final - target
    squares = jnp.sum(valid * jnp.sum(error * error, axis=1))
    grad_final = valid[:, None] * error * (total_tokens / count)
    grad_ffn_own = grad_final.astype(BF16)

    def reduce(left, right):
        whole = mm_tn(left, right).astype(BF16)
        size = whole.shape[0] // nb

        def part(slot):
            return lax.dynamic_slice_in_dim(whole, ring.owner(slot) * size, size)

        return ReduceRun(ring, order, part)

    (grad_ffn_own,) = gate(grad_ffn_own)
    near_ffn = Near(grad_ffn_own)
    d_gateup_all = jnp.zeros((length, 2 * WF), BF16)

    def ffn_back(whole, grad, at):
        d_hidden = mm_nt(grad, w_down)
        part = gateup[at : at + grad.shape[0]]
        gate_k, up_k = part[:, :WF], part[:, WF:]
        d_gate = (d_hidden * up_k * silu_slope(gate_k)).astype(BF16)
        d_up = (d_hidden * jax.nn.silu(gate_k)).astype(BF16)
        whole = lax.dynamic_update_slice(whole, d_gate, (at, 0))
        return lax.dynamic_update_slice(whole, d_up, (at, WF))

    d_gateup_all = ffn_back(d_gateup_all, near_ffn.own, 0)
    d_gateup_all = ffn_back(d_gateup_all, near_ffn.next, own)
    near_ffn.far, near_ffn.next, near_ffn.own, d_gateup_all = gate(
        near_ffn.far, near_ffn.next, near_ffn.own, d_gateup_all
    )
    near_ffn.cross()
    (near_ffn.last,) = gate(near_ffn.last)
    grad_ffn_all = stacked(near_ffn.blocks())
    d_gateup_all = ffn_back(d_gateup_all, near_rows(grad_ffn_all, True), 2 * own)
    r_down = reduce(hidden_all, grad_ffn_all)
    (d_gateup_all,) = gate(d_gateup_all)

    d_gateup_all = turn(r_down, d_gateup_all)
    held = [d_gateup_all]
    two = NearSum(lambda far: in_two(mm_nt(near_rows(held[0], far), w_gu)), 0, True)
    two.third, d_gateup_all = gate(two.third, d_gateup_all)
    held = [d_gateup_all]
    two.go()
    two.stay()
    two.first, two.near = turn(r_down, two.first, two.near)
    two.near, two.second = gate(two.near, two.second)
    grad_normed_two = two.result()
    w_two = norm_back(grad_normed_two, hidden_one, r_h, norm_second)
    g_norm_second = jnp.sum(grad_normed_two * hidden_one * r_h, axis=0)
    grad_hidden_one = grad_final + w_two
    branch_own = grad_hidden_one.astype(BF16)
    branch_own, grad_hidden_one, g_norm_second = gate(branch_own, grad_hidden_one, g_norm_second)
    near_branch = Near(branch_own)
    near_branch.next, d_gateup_all = turn(r_down, near_branch.next, d_gateup_all)
    r_gu = reduce(normed_two_all, d_gateup_all)
    near_branch.far = finish(r_down, near_branch.far)
    near_branch.cross()
    (near_branch.last,) = gate(near_branch.last)
    branch = absolute(near_branch.blocks(), j).reshape(length, MODEL_WIDTH)
    d_acts = mm_nt(branch, w_out)
    grad_attended = d_acts[:, WX:].astype(BF16)
    grad_gated = d_acts[:, :WX]
    grad_ssm_y = grad_gated * silu_z
    d_z = (grad_gated * ssm_y * silu_slope(gate_z)).astype(BF16)
    grad_attended, grad_ssm_y, d_z, branch = gate(grad_attended, grad_ssm_y, d_z, branch)

    out_whole = mm_tn(acts, branch).astype(BF16)

    def out_part(slot):
        b = home(ring.owner(slot))
        return jnp.concatenate(
            [
                lax.dynamic_slice_in_dim(out_whole, b * rows_out, rows_out),
                lax.dynamic_slice_in_dim(out_whole, WX + b * rows_attn, rows_attn),
            ],
            axis=0,
        )

    r_out = ReduceRun(ring, order, out_part)
    grad_attended = turn(r_gu, grad_attended)

    dq, dk, dv = attention_backward(queries, keys, values, segc, segr, grad_attended)
    sent = jnp.where(core == 0, dv, dk)
    d_kv_other = core_swap(sent)
    dq, dk, dv, d_kv_other = turn(r_out, dq, dk, dv, d_kv_other)
    d_query = turned(dq, cosine, -sine).astype(BF16)
    d_kv = jnp.where(core == 0, dk, dv) + d_kv_other
    d_kv = jnp.where(core == 0, turned(d_kv, cosine, -sine), d_kv).astype(BF16)
    d_second = jnp.concatenate([d_query, d_kv, d_z], axis=1)
    r_second = reduce(normed, d_second)

    def collected(run):
        return Collect(run.result.astype(BF16).reshape(NC, rows, run.result.shape[1]), j)

    grad_ssm_y, d_second = turn(r_gu, grad_ssm_y, d_second)
    d_early = mm_nt(d_second, w_second)
    operands = (grad_ssm_y, conv_x, saved, rest_ssd)
    d_in_x, dbc, d_raw, sums_a, tsums_a = ssd_backward(0, *operands)
    d_in_x, dbc, d_raw = turn(r_out, d_in_x, dbc, d_raw)
    d_in_x, dbc, d_raw = turn(r_second, d_in_x, dbc, d_raw)
    d_in_x, dbc, d_raw = turn(r_gu, d_in_x, dbc, d_raw)
    d_in_x, dbc, d_raw, sums_b, tsums_b = ssd_backward(1, *operands, (dbc, d_raw, d_in_x))
    d_in_x, dbc, d_raw = turn(r_second, d_in_x, dbc, d_raw)
    d_in_x, dbc, d_raw = turn(r_out, d_in_x, dbc, d_raw)
    d_bc = dbc.reshape(2, 2, length, WB)
    b_sum = NearSum(lambda far: d_bc[1 - upper if far else upper], core)
    b_sum.near = finish(r_gu, b_sum.near)
    col_gu = collected(r_gu)
    sums = sums_a + sums_b
    tsums = jnp.concatenate([tsums_a, tsums_b], axis=1)
    g_bias, g_log = sums[0, :HEADS], sums[1, :HEADS]
    g_taps_x = tsums[:TAPS]
    g_skip = jnp.sum(tsums[TAPS].reshape(HEADS, P_SIZE), axis=1)

    def conv_back(d_conv, value, taps):
        d_in = taps[0][None] * d_conv
        g_taps = [jnp.sum(d_conv * value, axis=0)]
        for lag in range(1, TAPS):
            masked = d_conv * keeps[lag]
            d_in = d_in + taps[lag][None] * shifted(masked, -lag)
            g_taps.append(jnp.sum(masked * shifted(value, lag), axis=0))
        return d_in.astype(BF16), jnp.stack(g_taps)

    b_sum.second, b_sum.near, b_sum.first, conv_b_own, taps_b_own, col_gu.got = turn(
        r_second, b_sum.second, b_sum.near, b_sum.first, conv_b_own, taps_b_own, col_gu.got
    )
    col_gu.cross()
    conv_b_wide = conv_b_own.astype(F32)
    conv_out_b = convolve(conv_b_wide, taps_b_own, keeps)
    d_in_b, g_taps_b = conv_back(b_sum.result() * silu_slope(conv_out_b), conv_b_wide, taps_b_own)
    d_first = jnp.concatenate(
        [d_in_x, d_in_b, d_raw.astype(BF16)], axis=1
    )
    r_first = reduce(normed, d_first)
    d_first = finish(r_out, d_first)
    d_first, col_gu.far = finish(r_second, d_first, col_gu.far)
    col_second = collected(r_second)
    d_first, col_second.got, out_kept = turn(
        r_first, d_first, col_second.got, r_out.result.astype(BF16)
    )
    col_second.cross()
    out_home = lax.ppermute(out_kept, ("batch", "ctx"), back)

    held = [d_first]
    gain_parts = []

    def normed_part(far):
        addends = in_two(mm_nt(upper_rows(held[0], far), w_first) + upper_rows(d_early, far))
        scaled = upper_rows(normed, far).astype(F32).reshape(addends.shape)
        gain_parts.append(jnp.sum(addends * scaled, axis=(0, 1)))
        return addends

    back_sum = NearSum(normed_part, core, True)
    back_sum.third, d_first = turn(r_first, back_sum.third, d_first)
    held = [d_first]
    back_sum.go()
    back_sum.stay()
    g_norm_first = (gain_parts[0] + gain_parts[1]) / norm_first
    back_sum.near, g_norm_first, col_second.far, out_home = turn(
        r_first, back_sum.near, g_norm_first, col_second.far, out_home
    )
    taps_all = jnp.zeros((TAPS, DI + 2 * N), F32)
    taps_all = lax.dynamic_update_slice(taps_all, g_taps_x, (0, j * WX))
    taps_all = lax.dynamic_update_slice(taps_all, g_taps_b, (0, DI + j * WB))
    per_head = lax.dynamic_update_slice(
        jnp.zeros((3, 128), F32), jnp.stack([g_log, g_skip, g_bias]), (0, heads_at)
    )
    small = jnp.concatenate(
        [
            g_norm_first.reshape(-1, 128),
            g_norm_second.reshape(-1, 128),
            taps_all.reshape(-1, 128),
            per_head,
            jnp.broadcast_to(squares, (1, 128)),
        ]
    )
    moves = [("batch", nb, 1 << q) for q in range(nb.bit_length() - 1)]
    moves += [("ctx", NC, 1), ("ctx", NC, 2)]
    for axis, size, bit in moves:
        small = small + lax.ppermute(small, axis, [(q, q ^ bit) for q in range(size)])
    back_sum.first = finish(r_first, back_sum.first)
    col_first = collected(r_first)
    back_sum.second, back_sum.first, col_first.got = gate(
        back_sum.second, back_sum.first, col_first.got
    )
    col_first.cross()
    grad_normed = back_sum.result()
    grad_tokens = grad_hidden_one + norm_back(grad_normed, x, r_x, norm_first)
    small, grad_tokens = gate(small, grad_tokens)
    lines = MODEL_WIDTH // 128
    g_norm_first = small[:lines].reshape(MODEL_WIDTH)
    g_norm_second = small[lines : 2 * lines].reshape(MODEL_WIDTH)
    taps_all = small[2 * lines : -4].reshape(TAPS, DI + 2 * N)
    per_head = small[-4:-1, :H_M]
    loss_value = small[-1, 0] / (MODEL_WIDTH * count) + order.token[0, 0]

    got_gu = col_gu.result()
    grad_gate_up = (
        got_gu.reshape(NC, rows, 2, nb, unit).transpose(1, 2, 3, 0, 4).reshape(rows, 2 * FF)
    )
    got_second = col_second.result()
    got_first = col_first.result()

    def columns(got, begin, size):
        return got[:, :, begin : begin + size].transpose(1, 0, 2).reshape(rows, NC * size)

    grad_query = columns(got_second, 0, WQ)
    grad_keyval = (
        got_second[:, :, WQ : WQ + HEAD_SIZE]
        .reshape(2, 2, rows, HEAD_SIZE)
        .transpose(2, 1, 0, 3)
        .reshape(rows, 4 * HEAD_SIZE)
    )
    grad_mixer_in = jnp.concatenate(
        [
            columns(got_second, WQ + HEAD_SIZE, WX),
            columns(got_first, 0, WX),
            columns(got_first, WX, WB),
            columns(got_first, WX + WB, HEADS),
        ],
        axis=1,
    )
    output = final.astype(BF16).reshape(tokens.shape)
    return (
        output,
        loss_value,
        grad_tokens.reshape(tokens.shape),
        grad_mixer_in,
        out_home[:rows_out].astype(F32),
        grad_query,
        grad_keyval,
        out_home[rows_out:].astype(F32),
        grad_gate_up,
        r_down.result,
        g_norm_first,
        g_norm_second,
        taps_all,
        per_head[0],
        per_head[1],
        per_head[2],
    )


def solution(mesh):
    split_rows = P(("batch", "ctx"), None)
    by_token = P("batch", "ctx", None)
    return jax.shard_map(
        body,
        mesh=mesh,
        in_specs=(by_token, P("batch", "ctx"), P("batch", "ctx"), by_token)
        + (split_rows,) * 7
        + (P(),) * 6,
        out_specs=(by_token, P(), by_token) + (split_rows,) * 7 + (P(),) * 6,
        check_vma=False,
    )
```
